128 devices in a mesh: alpha: 8 (over x, core), beta: 16 (over z, y).
Axes of the slice: x: 4, y: 4, z: 4, core: 2. Of those that a mesh axis runs over, the one named last changes fastest.
Arguments:
- csf_coef: float32 [42, 98304], P(None, ('alpha', 'beta')), may hold values from -18 to 18
- conf_class: int32 [98304], P(('alpha', 'beta')), may hold values from 0 to 5
- conf_tile: int32 [98304, 1], P(('alpha', 'beta')), may hold values from 0 to 127, as said below
- transforms: float32 [6, 42, 256], replicated, may hold values from -1 to 1
- alpha_targets: int32 [16, 12288], P(None, 'alpha'), may hold values from 0 to 12287, as said below
- alpha_values: bfloat16 [16, 12288], P(None, 'alpha'), may hold values from -1.796875 to 1.796875
- alpha_counts: int32 [12288], P('alpha'), may hold values from 1 to 16, as said below
- beta_targets: int32 [16, 6144], P(None, 'beta'), may hold values from 0 to 6143, as said below
- beta_values: bfloat16 [16, 6144], P(None, 'beta'), may hold values from -1.796875 to 1.796875
- beta_counts: int32 [6144], P('beta'), may hold values from 1 to 16, as said below
- det_diag: float32 [12288, 6144], P('alpha', 'beta'), may hold values from 0.5 to 2
Outputs:
- residual: float32 [42, 98304], P(None, ('alpha', 'beta'))
- residual_rms: float32 [], replicated
The draws below stay inside these ranges and needn't reach their ends.
Inputs may be any that keep to these rules, and one draw needn't show every extreme that they name: `conf_tile`: among the 768 configurations of one device no tile is named more than 18 times; in every draw some tile is named exactly 18 times by the configurations of every device. `alpha_targets`: in each column the 16 entries are distinct and differ from the column's own string. `beta_targets`: in each column the 16 entries are distinct and differ from the column's own string. `alpha_counts`: some string has exactly 16. `beta_counts`: some string has exactly 16.
All inputs are finite; a program needn't handle non-finite values.
Results may differ from the reference program's by a relative error of at most 0.00075.
The reference program's roundings to bfloat16 on the way (of `det_values`, `amplitude`, `sigma_grid` and `sigma_dets`) count: a program that leaves them out, or rounds other values in their place, can miss the bound.
Values may be sent and summed in bfloat16 or wider, within the bound.
No kernel may reach another device: no remote copies, remote signals or barrier semaphores. Data moves between devices by JAX's collectives and lax.ppermute only.
A program may use at most 128 MiB of HBM per device.

```python
import jax
import jax.numpy as jnp
from jax import lax

NCSF = 42
NDET = 256
CLASSES = 6
EXC = 16
CONF_DEV = 768
TB = 384
TA = 1536
CONFIGS = 98304
NA = 12288
NB = 6144
N_ALPHA = 8
N_BETA = 16


def draw_csf_coef(key, part):
    position = jnp.arange(CONFIGS, dtype=jnp.float32) / max(CONFIGS - 1, 1)
    scales = 1.0 + 2.0 * position
    base_draw = jnp.clip(jax.random.normal(key, (NCSF, CONFIGS), jnp.float32), -6.0, 6.0)
    return base_draw * scales[None, :]


def draw_conf_tile(key, part):
    devices = N_ALPHA * N_BETA
    capacity = 3 * CONF_DEV // devices
    full_tile = jax.random.randint(jax.random.fold_in(key, 1000001), (), 0, devices)
    popularity = jax.random.randint(jax.random.fold_in(key, 1000002), (devices,), 0, 4)
    candidate = jnp.arange(devices * capacity, dtype=jnp.int32)
    owner_tile = candidate // capacity

    def one_sender(sender):
        sender_key = jax.random.fold_in(key, sender)
        noise_bits = jax.random.randint(jax.random.fold_in(sender_key, 1), (devices * capacity,), 0, 65536)
        scores = noise_bits + popularity[owner_tile] * 24000
        scores = jnp.where(owner_tile == full_tile, -1, scores)
        scores = scores * (devices * capacity) + candidate
        picked = lax.top_k(scores, CONF_DEV - capacity)[1]
        chosen = jnp.concatenate([jnp.full((capacity,), full_tile, jnp.int32), owner_tile[picked]])
        shuffle = jax.random.permutation(jax.random.fold_in(sender_key, 2), CONF_DEV)
        return chosen[shuffle]
    routing = jax.vmap(one_sender)(jnp.arange(devices, dtype=jnp.int32))
    return routing.reshape(CONFIGS, 1).astype(jnp.int32)


def coupling_targets(key, length):
    slot = jnp.arange(EXC, dtype=jnp.int32)[:, None]
    band_lo = 1 + slot * (length - 1) // EXC
    band_hi = 1 + (slot + 1) * (length - 1) // EXC
    band_lo = jnp.broadcast_to(band_lo, (EXC, length))
    band_hi = jnp.broadcast_to(band_hi, (EXC, length))
    offsets = jax.random.randint(jax.random.fold_in(key, 1), (EXC, length), band_lo, band_hi)
    return ((jnp.arange(length, dtype=jnp.int32)[None, :] + offsets) % length).astype(jnp.int32)


def occupancy(key, length):
    base_draw = jax.random.randint(jax.random.fold_in(key, 1), (length,), 1, EXC + 1)
    where_full = jax.random.randint(jax.random.fold_in(key, 2), (), 0, length)
    return base_draw.at[where_full].set(EXC).astype(jnp.int32)


def draw_alpha_targets(key, part):
    return coupling_targets(jax.random.fold_in(key, 31), NA)


def draw_beta_targets(key, part):
    return coupling_targets(jax.random.fold_in(key, 32), NB)


def draw_alpha_counts(key, part):
    return occupancy(jax.random.fold_in(key, 41), NA)


def draw_beta_counts(key, part):
    return occupancy(jax.random.fold_in(key, 42), NB)


def with_ends(array, rng, low, high):
    index_at = [jax.random.randint(jax.random.fold_in(rng, axis), (), 0, length) for axis, length in enumerate(array.shape)]
    longest = array.shape.index(max(array.shape))
    beside = index_at[:longest] + [(index_at[longest] + 1) % array.shape[longest]] + index_at[longest + 1:]
    return array.at[tuple(index_at)].set(low).at[tuple(beside)].set(high)


def levels(key, extent, pieces, least, top_value):
    loudness, own = 1.0, jax.random.fold_in(key, 6)
    for dim, parts in pieces:
        draws = jnp.exp(jax.random.uniform(jax.random.fold_in(own, dim), (parts,), jnp.float32, least / len(pieces), top_value / len(pieces)))
        loudness = loudness * jnp.repeat(draws, extent[dim] // parts).reshape([-1 if axis == dim else 1 for axis in range(len(extent))])
    return loudness


def noise(rng, extent, spread, bound, split=(), held_as=jnp.bfloat16):
    level = levels(rng, extent, split, -0.22, 0.18) if split else 1.0
    values = jax.random.normal(rng, extent, jnp.float32) * spread * level
    return jnp.minimum(jnp.maximum(values, -bound), bound).astype(held_as)


def setup_inputs(seed: int = 0) -> dict:
    seeds = jax.random.split(jax.random.key(seed), 12)
    csf_coef = draw_csf_coef(jax.random.fold_in(seeds[11], 71), 0)
    conf_class = with_ends(jax.random.randint(seeds[1], (CONFIGS,), 0, CLASSES), jax.random.fold_in(seeds[1], 1), 0, CLASSES - 1).astype(jnp.int32)
    conf_tile = draw_conf_tile(jax.random.fold_in(seeds[11], 71), 0)
    transforms = noise(seeds[3], (CLASSES, NCSF, NDET), NCSF ** -0.5, 1.0, (), jnp.float32)
    alpha_targets = draw_alpha_targets(jax.random.fold_in(seeds[11], 71), 0)
    alpha_values = noise(seeds[5], (EXC, NA), 0.3, 1.796875, ((1, 8),))
    alpha_counts = draw_alpha_counts(jax.random.fold_in(seeds[11], 71), 0)
    beta_targets = draw_beta_targets(jax.random.fold_in(seeds[11], 71), 0)
    beta_values = noise(seeds[8], (EXC, NB), 0.3, 1.796875, ((1, 16),))
    beta_counts = draw_beta_counts(jax.random.fold_in(seeds[11], 71), 0)
    det_diag = jnp.clip(0.5 + 1.5 * jax.random.uniform(seeds[10], (NA, NB), jnp.float32) ** levels(seeds[10], (NA, NB), ((0, 8), (1, 16)), -0.2, 0.2), 0.5, 2.0)
    return dict(csf_coef=csf_coef, conf_class=conf_class, conf_tile=conf_tile, transforms=transforms, alpha_targets=alpha_targets, alpha_values=alpha_values, alpha_counts=alpha_counts, beta_targets=beta_targets, beta_values=beta_values, beta_counts=beta_counts, det_diag=det_diag)


def class_forward(coefs, classes, transforms):
    summed = jnp.zeros((coefs.shape[1], transforms.shape[2]), jnp.float32)
    for class_id in range(transforms.shape[0]):
        masked = jnp.where(classes[None, :] == class_id, coefs, jnp.zeros_like(coefs))
        summed = summed + lax.dot_general(masked, transforms[class_id], (((0,), (0,)), ((), ())), precision=lax.Precision.HIGHEST, preferred_element_type=jnp.float32)
    return summed

def class_backward(values, classes, transforms):
    summed = jnp.zeros((transforms.shape[1], values.shape[0]), jnp.float32)
    for class_id in range(transforms.shape[0]):
        product = lax.dot_general(transforms[class_id], values, (((1,), (1,)), ((), ())), precision=lax.Precision.HIGHEST, preferred_element_type=jnp.float32)
        summed = summed + jnp.where(classes[None, :] == class_id, product, jnp.zeros_like(product))
    return summed

def bucket_slots(chosen_tiles, buckets):
    onehot = (chosen_tiles[:, None] == jnp.arange(buckets, dtype=jnp.int32)[None, :]).astype(jnp.int32)
    running = jnp.cumsum(onehot, axis=0) - onehot
    return lax.optimization_barrier(jnp.sum(onehot * running, axis=1)).astype(jnp.int32)

def live_weights(values, counts):
    active = jnp.arange(values.shape[0], dtype=jnp.int32)[:, None] < counts[None, :]
    return jnp.where(active, values.astype(jnp.float32), jnp.zeros(values.shape, jnp.float32))

def reference(csf_coef, conf_class, conf_tile, transforms, alpha_targets, alpha_values, alpha_counts, beta_targets, beta_values, beta_counts, det_diag):
    devices = N_ALPHA * N_BETA
    capacity = 3 * CONF_DEV // devices
    target_tile = conf_tile[:, 0].astype(jnp.int32)
    slot_index = lax.map(lambda chosen: bucket_slots(chosen, devices), target_tile.reshape(devices, CONF_DEV)).reshape(CONFIGS).astype(jnp.int32)
    sender = (jnp.arange(CONFIGS, dtype=jnp.int32) // CONF_DEV).astype(jnp.int32)
    group_index = (sender * capacity + slot_index).astype(jnp.int32)
    det_values = class_forward(csf_coef, conf_class, transforms).astype(jnp.bfloat16)
    tiles = jnp.zeros((devices, devices * capacity, NDET), jnp.bfloat16).at[target_tile, group_index].set(det_values)
    amplitude = tiles.reshape(N_ALPHA, N_BETA, TA, TB).transpose(0, 2, 1, 3).reshape(NA, NB)
    amp_float = amplitude.astype(jnp.float32)
    alpha_live = live_weights(alpha_values, alpha_counts)
    beta_live = live_weights(beta_values, beta_counts)

    def alpha_step(excitation, summed):
        return summed + alpha_live[excitation][:, None] * amp_float[alpha_targets[excitation]]

    def beta_step(excitation, summed):
        return summed + beta_live[excitation][None, :] * amp_float[:, beta_targets[excitation]]
    alpha_term = lax.fori_loop(0, EXC, alpha_step, jnp.zeros((NA, NB), jnp.float32))
    beta_term = lax.fori_loop(0, EXC, beta_step, jnp.zeros((NA, NB), jnp.float32))
    sigma_grid = (alpha_term + beta_term + det_diag * amp_float).astype(jnp.bfloat16)
    sigma_tiles = sigma_grid.reshape(N_ALPHA, TA, N_BETA, TB).transpose(0, 2, 1, 3).reshape(devices, devices * capacity, NDET)
    sigma_dets = sigma_tiles[target_tile, group_index].astype(jnp.float32)
    sigma_csf = class_backward(sigma_dets, conf_class, transforms)
    rayleigh = jnp.sum(csf_coef * sigma_csf) / jnp.sum(csf_coef * csf_coef)
    residual = sigma_csf - rayleigh * csf_coef
    residual_rms = jnp.sqrt(jnp.sum(residual * residual) / (NCSF * CONFIGS))
    return (residual, residual_rms)
```

```python
import functools

import jax
import jax.numpy as jnp
from jax import lax
from jax.experimental import pallas as pl
from jax.experimental.pallas import tpu as pltpu
from jax.sharding import PartitionSpec as P

F32 = jnp.float32
BF16 = jnp.bfloat16
HIGH = lax.Precision.HIGHEST
BOTH = ("alpha", "beta")
PAD = 8
VMEM_LIMIT = 60 * 1024 * 1024


def masked_coefs(coef, classes, classes_n, width):
    parts = []
    for c in range(classes_n):
        parts.append(jnp.where(classes == c, coef, jnp.zeros_like(coef)))
    return jnp.concatenate(parts, axis=0)


def pack_kernel(capacity, coef_ref, class_ref, tile_ref, tr_ref, out_ref, key_ref, inter_ref):
    confs = coef_ref.shape[1]
    ncls = tr_ref.shape[0] // coef_ref.shape[0]
    devices = confs * 3 // capacity
    masked = masked_coefs(coef_ref[...], class_ref[...], ncls, confs)
    dets = lax.dot_general(
        masked, tr_ref[...], (((0,), (0,)), ((), ())), precision=HIGH, preferred_element_type=F32
    ).astype(BF16)
    tile = tile_ref[...]
    hit = lax.broadcasted_iota(jnp.int32, (devices, confs), 0) == tile
    before = lax.broadcasted_iota(jnp.int32, (confs, confs), 0) < lax.broadcasted_iota(
        jnp.int32, (confs, confs), 1
    )
    counts = jnp.dot(
        hit.astype(F32).astype(BF16), before.astype(F32).astype(BF16), preferred_element_type=F32
    )
    slot = jnp.sum(jnp.where(hit, counts, 0.0), axis=0, keepdims=True).astype(jnp.int32)
    key = tile * capacity + slot
    key_ref[...] = key
    rows = devices * capacity
    block = 256
    for b in range(rows // block):
        onehot = (
            (lax.broadcasted_iota(jnp.int32, (block, confs), 0) + b * block == key)
            .astype(F32)
            .astype(BF16)
        )
        picked = jnp.dot(onehot, dets, preferred_element_type=F32)
        for h in range(2):
            inter_ref[pl.ds(h, block, stride=2), :] = picked[:, h * 128 : (h + 1) * 128]
        out_ref[pl.ds(b * 2 * block, 2 * block), :] = inter_ref[...].astype(BF16)


def pack(coef48, classes, tiles, tr, capacity):
    confs = coef48.shape[1]
    rows = 2 * 3 * confs
    return pl.pallas_call(
        functools.partial(pack_kernel, capacity),
        out_shape=(
            jax.ShapeDtypeStruct((rows, 128), BF16),
            jax.ShapeDtypeStruct((1, confs), jnp.int32),
        ),
        scratch_shapes=[pltpu.VMEM((512, 128), F32)],
        compiler_params=pltpu.CompilerParams(vmem_limit_bytes=VMEM_LIMIT),
        name="pack",
    )(coef48, classes, tiles, tr)


def beta_kernel(x_ref, tgt_ref, w_ref, out_ref, table_ref, wt_ref, acc_ref, stage_ref):
    blocks = x_ref.shape[0]
    rows = x_ref.shape[1]
    lanes = rows // 3

    @pl.when(pl.program_id(0) == 0)
    def _():
        def build(j, carry):
            stage_ref[...] = x_ref[j].astype(F32)
            for ct in range(3):
                piece = stage_ref[pl.ds(ct, lanes, stride=3), :]
                piece = jnp.concatenate([piece, jnp.zeros((128 - lanes, 128), F32)], axis=0)
                start = pl.multiple_of((j * 3 + ct) * 128 + PAD, 8)
                table_ref[pl.ds(start, 128), :] = piece.T
            return carry

        lax.fori_loop(0, blocks, build, 0)

    sub = lax.broadcasted_iota(jnp.int32, (8, 128), 0)
    for ct in range(3):
        wt_ref[...] = jnp.concatenate(
            [w_ref[0, pl.ds(ct, 16, stride=3), :], jnp.zeros((112, 128), F32)], axis=0
        ).T

        def group(g, carry):
            first = g * 8
            w8 = wt_ref[pl.ds(pl.multiple_of(first, 8), 8), :]
            acc = jnp.zeros((8, 128), F32)
            for e in range(16):
                got = None
                for s in range(8):
                    t = tgt_ref[0, e * 3 + ct, first + s]
                    win = table_ref[pl.ds(t + (PAD - s), 8), :]
                    got = win if s == 0 else jnp.where(sub == s, win, got)
                acc = acc + got * w8[:, e : e + 1]
            acc_ref[pl.ds(pl.multiple_of(first, 8), 8), :] = acc
            return carry

        lax.fori_loop(0, 16, group, 0)
        out_ref[0, pl.ds(ct, lanes, stride=3), :] = acc_ref[...].T[:lanes]


def beta_term(x2, targets, weights):
    blocks, rows, _ = x2.shape
    cols = blocks * 384
    return pl.pallas_call(
        beta_kernel,
        out_shape=jax.ShapeDtypeStruct((blocks, rows, 128), F32),
        grid=(blocks,),
        in_specs=[
            pl.BlockSpec((blocks, rows, 128), lambda j: (0, 0, 0)),
            pl.BlockSpec((1, 48, 128), lambda j: (j, 0, 0), memory_space=pltpu.SMEM),
            pl.BlockSpec((1, 48, 128), lambda j: (j, 0, 0)),
        ],
        out_specs=pl.BlockSpec((1, rows, 128), lambda j: (j, 0, 0)),
        scratch_shapes=[
            pltpu.VMEM((cols + 2 * PAD, 128), F32),
            pltpu.VMEM((128, 128), F32),
            pltpu.VMEM((128, 128), F32),
            pltpu.VMEM((rows, 128), F32),
        ],
        compiler_params=pltpu.CompilerParams(vmem_limit_bytes=VMEM_LIMIT),
        cost_estimate=pl.CostEstimate(
            flops=2 * cols * 16 * 1024, bytes_accessed=8 * 2**20, transcendentals=0
        ),
        name="beta_term",
    )(x2, targets, weights)


def alpha_kernel(
    nsend, own_ref, tbl_hbm, tgt_ref, w_ref, diag_ref, out_ref, table_ref, dpiece_ref, buf_ref, sem
):
    chunk = buf_ref.shape[1]
    total = tbl_hbm.shape[0]
    n = total // chunk

    def fetch(k, slot):
        return pltpu.make_async_copy(
            tbl_hbm.at[pl.ds(pl.multiple_of(k * chunk, 16), chunk), :],
            buf_ref.at[slot],
            sem.at[slot],
        )

    fetch(0, 0).start()
    rows = diag_ref.shape[0]

    def interleave(k, carry):
        base = pl.multiple_of(k * 8, 8)
        for ct in range(3):
            dpiece_ref[pl.ds(base * 3 + ct, 8, stride=3), :] = diag_ref[
                pl.ds(base, 8), ct * 128 : (ct + 1) * 128
            ]
        return carry

    lax.fori_loop(0, rows // 8, interleave, 0)

    def load(k, carry):
        slot = lax.rem(k, 2)

        @pl.when(k + 1 < n)
        def _():
            fetch(k + 1, 1 - slot).start()

        fetch(k, slot).wait()
        table_ref[pl.ds(pl.multiple_of(k * chunk, 8), chunk), :] = buf_ref[slot].astype(F32)
        return carry

    lax.fori_loop(0, n, load, 0)
    per = rows // nsend
    own = own_ref[0]
    halves = nsend // 16

    def sender(k, carry):
        beta_s = k // halves
        alpha_s = k - beta_s * halves
        nat = (alpha_s * 16 + beta_s) * per
        pos = k * per
        for r in range(per):
            a = nat + r
            o = (pos + r) * 3
            acc = jnp.zeros((8, 128), F32)
            for e in range(16):
                acc = acc + table_ref[pl.ds(tgt_ref[e, a], 8), :] * w_ref[e, a]
            acc = acc + dpiece_ref[pl.ds(a * 3, 8), :] * table_ref[pl.ds(own + o, 8), :]
            out_ref[pl.ds(o, 8), :] = acc
        return carry

    lax.fori_loop(0, nsend, sender, 0)


def alpha_term(own, table, targets, weights, diag, nsend):
    rows = diag.shape[0]
    total = table.shape[0]
    chunk = total // 16
    return pl.pallas_call(
        functools.partial(alpha_kernel, nsend),
        out_shape=jax.ShapeDtypeStruct((rows * 3 + PAD, 128), F32),
        in_specs=[
            pl.BlockSpec(memory_space=pltpu.SMEM),
            pl.BlockSpec(memory_space=pl.ANY),
            pl.BlockSpec(memory_space=pltpu.SMEM),
            pl.BlockSpec(memory_space=pltpu.SMEM),
            pl.BlockSpec(memory_space=pltpu.VMEM),
        ],
        out_specs=pl.BlockSpec(memory_space=pltpu.VMEM),
        scratch_shapes=[
            pltpu.VMEM((total + PAD, 128), F32),
            pltpu.VMEM((rows * 3 + PAD, 128), F32),
            pltpu.VMEM((2, chunk, 128), BF16),
            pltpu.SemaphoreType.DMA((2,)),
        ],
        compiler_params=pltpu.CompilerParams(vmem_limit_bytes=VMEM_LIMIT),
        name="alpha_term",
    )(own, table, targets, weights, diag)


def unpack_kernel(
    r_ref, key_ref, class_ref, coef_ref, tr_ref, sigma_ref, part_ref, stage_ref, half_ref
):
    rows2 = r_ref.shape[0]
    rows = rows2 // 2
    confs = key_ref.shape[1]
    width = coef_ref.shape[0]
    ncls = tr_ref.shape[0] // width
    stage_ref[...] = r_ref[...].astype(F32)
    for h in range(2):
        half_ref[:, h * 128 : (h + 1) * 128] = stage_ref[pl.ds(h, rows, stride=2), :].astype(BF16)
    key = key_ref[...]
    block = 256
    dets = jnp.zeros((256, confs), F32)
    for b in range(rows // block):
        onehot = (
            (lax.broadcasted_iota(jnp.int32, (block, confs), 0) + b * block == key)
            .astype(F32)
            .astype(BF16)
        )
        dets = dets + lax.dot_general(
            half_ref[pl.ds(b * block, block), :],
            onehot,
            (((0,), (0,)), ((), ())),
            preferred_element_type=F32,
        )
    products = jnp.dot(tr_ref[...], dets, precision=HIGH, preferred_element_type=F32)
    sigma = jnp.zeros((width, confs), F32)
    for c in range(ncls):
        sigma = sigma + jnp.where(class_ref[...] == c, products[c * width : (c + 1) * width], 0.0)
    coef = coef_ref[...]
    sigma_ref[...] = sigma
    square = jnp.sum(jnp.sum(coef * coef, axis=1, keepdims=True), axis=0, keepdims=True)
    cross = jnp.sum(jnp.sum(coef * sigma, axis=1, keepdims=True), axis=0, keepdims=True)
    ratio = jnp.where(square > 0.0, cross / jnp.where(square > 0.0, square, 1.0), 0.0)
    rest = sigma - ratio * coef
    rho = jnp.sum(jnp.sum(rest * rest, axis=1, keepdims=True), axis=0, keepdims=True)
    lane = lax.broadcasted_iota(jnp.int32, (1, 128), 1)
    part_ref[...] = jnp.where(
        lane == 0,
        square,
        jnp.where(lane == 1, cross, jnp.where(lane == 2, rho, jnp.where(lane == 3, ratio, 0.0))),
    )


def unpack(returned, key, classes, coef48, tr):
    confs = coef48.shape[1]
    return pl.pallas_call(
        unpack_kernel,
        out_shape=(
            jax.ShapeDtypeStruct(coef48.shape, F32),
            jax.ShapeDtypeStruct((1, 128), F32),
        ),
        scratch_shapes=[
            pltpu.VMEM(returned.shape, F32),
            pltpu.VMEM((returned.shape[0] // 2, 256), BF16),
        ],
        compiler_params=pltpu.CompilerParams(vmem_limit_bytes=VMEM_LIMIT),
        name="unpack",
    )(returned, key, classes, coef48, tr)


def exchange(x, axes):
    return lax.all_to_all(x, axes, split_axis=0, concat_axis=0, tiled=True)


def body(
    csf_coef,
    conf_class,
    conf_tile,
    transforms,
    alpha_targets,
    alpha_values,
    alpha_counts,
    beta_targets,
    beta_values,
    beta_counts,
    det_diag,
):
    nalpha = lax.axis_size("alpha")
    nbeta = lax.axis_size("beta")
    devices = nalpha * nbeta
    ncsf, confs = csf_coef.shape
    capacity = 3 * confs // devices
    rows_alpha, cols_beta = det_diag.shape
    classes_n, _, width = transforms.shape
    exc = alpha_targets.shape[0]
    pieces = capacity * width // 128
    per = pieces * 128 // cols_beta
    csf_pad = -ncsf % 8
    coef48 = jnp.pad(csf_coef, ((0, csf_pad), (0, 0)))
    tr = jnp.pad(transforms, ((0, 0), (0, csf_pad), (0, 0))).reshape(-1, width)
    classes = conf_class[None, :]
    tiles = conf_tile[:, 0][None, :]

    slots = jnp.arange(exc, dtype=jnp.int32)[:, None]
    live_beta = jnp.where(slots < beta_counts[None, :], beta_values, jnp.zeros_like(beta_values))
    lists = jnp.concatenate(
        [
            (beta_targets // 128).astype(BF16).reshape(-1, 128),
            (beta_targets % 128).astype(BF16).reshape(-1, 128),
            live_beta.reshape(-1, 128),
        ],
        axis=0,
    )

    outgoing, key = pack(coef48, classes, tiles, tr, capacity)
    slab = exchange(outgoing.reshape(nalpha, nbeta * pieces, 128), "alpha")
    x2 = (
        slab.reshape(nalpha, nbeta, pieces, 128)
        .transpose(1, 0, 2, 3)
        .reshape(nbeta, nalpha * pieces, 128)
    )
    sent = jnp.concatenate(
        [x2, jnp.broadcast_to(lists[None], (nbeta,) + lists.shape)], axis=1
    )
    got = exchange(sent, "beta")
    body_rows = nalpha * pieces
    tile = got[:, :body_rows].reshape(-1, 128)
    lrows = lists.shape[0] // 3
    high = got[:, body_rows : body_rows + lrows].astype(jnp.int32)
    low = got[:, body_rows + lrows : body_rows + 2 * lrows].astype(jnp.int32)
    btargets = high * 128 + low
    bweights = got[:, body_rows + 2 * lrows :].astype(F32)

    table = lax.all_gather(tile, "alpha", axis=0, tiled=True)
    beta_slab = beta_term(x2, btargets, bweights)

    owner = alpha_targets // rows_alpha
    inner = alpha_targets % rows_alpha
    sender = inner // per
    row = inner % per
    place = ((sender % nbeta) * nalpha + sender // nbeta) * per + row
    atargets = (owner * rows_alpha + place) * (cols_beta // 128)
    aweights = jnp.where(slots < alpha_counts[None, :], alpha_values.astype(F32), 0.0)
    own = (lax.axis_index("alpha") * (rows_alpha * cols_beta // 128)).astype(jnp.int32)[None]
    partial = alpha_term(own, table, atargets, aweights, det_diag, devices)
    partial = partial[: rows_alpha * 3].reshape(nbeta, body_rows, 128)
    passed = exchange(partial, "beta")
    sigma_slab = (
        (passed + beta_slab)
        .astype(BF16)
        .reshape(nbeta, nalpha, pieces, 128)
        .transpose(1, 0, 2, 3)
        .reshape(nalpha, nbeta * pieces, 128)
    )
    returned = exchange(sigma_slab, "alpha").reshape(-1, 128)
    sigma48, part = unpack(returned, key, classes, coef48, tr)
    parts = exchange(jnp.broadcast_to(part[None], (devices, 1, 128)), BOTH)[:, 0]
    square = parts[:, 0]
    rayleigh = jnp.sum(parts[:, 1]) / jnp.sum(square)
    shift = rayleigh - parts[:, 3]
    residual_square = jnp.sum(parts[:, 2] + shift * shift * square)
    residual = sigma48[:ncsf] - rayleigh * csf_coef
    residual_rms = jnp.sqrt(residual_square / (ncsf * confs * devices))
    return (residual, residual_rms)


def solution(mesh):
    placed = (
        P(None, BOTH),
        P(BOTH),
        P(BOTH, None),
        P(),
        P(None, "alpha"),
        P(None, "alpha"),
        P("alpha"),
        P(None, "beta"),
        P(None, "beta"),
        P("beta"),
        P("alpha", "beta"),
    )
    return jax.shard_map(
        body,
        mesh=mesh,
        in_specs=placed,
        out_specs=(P(None, BOTH), P()),
        check_vma=False,
    )
```

```python
import functools

import jax
import jax.numpy as jnp
from jax import lax
from jax.experimental import pallas as pl
from jax.experimental.pallas import tpu as pltpu
from jax.sharding import PartitionSpec as P

F32 = jnp.float32
BF16 = jnp.bfloat16
HIGH = lax.Precision.HIGHEST
BOTH = ("alpha", "beta")
PAD = 8
FIRST = 5
STEPS = 2
VMEM_LIMIT = 60 * 1024 * 1024


def stacked(coef, classes, classes_n):
    parts = []
    for c in range(classes_n):
        parts.append(jnp.where(classes == c, coef, jnp.zeros_like(coef)))
    return jnp.concatenate(parts, axis=0)


def padded(ref, index=None):
    value = ref[...] if index is None else ref[index]
    fill = -value.shape[0] % 8
    return jnp.concatenate([value, jnp.zeros((fill, value.shape[1]), F32)], axis=0)


def pack_kernel(capacity, coef_ref, label_ref, tr_ref, out_ref, key_ref, inter_ref):
    confs = coef_ref.shape[1]
    ncls = tr_ref.shape[0]
    devices = confs * 3 // capacity
    masked = stacked(padded(coef_ref), label_ref[0:1, :], ncls)
    trans = jnp.concatenate([padded(tr_ref, c) for c in range(ncls)], axis=0)
    dets = lax.dot_general(
        masked, trans, (((0,), (0,)), ((), ())), precision=HIGH, preferred_element_type=F32
    ).astype(BF16)
    tile = label_ref[1:2, :]
    hit = lax.broadcasted_iota(jnp.int32, (devices, confs), 0) == tile
    before = lax.broadcasted_iota(jnp.int32, (confs, confs), 0) < lax.broadcasted_iota(
        jnp.int32, (confs, confs), 1
    )
    counts = jnp.dot(
        hit.astype(F32).astype(BF16), before.astype(F32).astype(BF16), preferred_element_type=F32
    )
    slot = jnp.sum(jnp.where(hit, counts, 0.0), axis=0, keepdims=True).astype(jnp.int32)
    key = tile * capacity + slot
    key_ref[...] = key
    rows = devices * capacity
    block = 256
    for b in range(rows // block):
        onehot = (
            (lax.broadcasted_iota(jnp.int32, (block, confs), 0) + b * block == key)
            .astype(F32)
            .astype(BF16)
        )
        picked = jnp.dot(onehot, dets, preferred_element_type=F32)
        for h in range(2):
            inter_ref[pl.ds(h, block, stride=2), :] = picked[:, h * 128 : (h + 1) * 128]
        out_ref[pl.ds(b * 2 * block, 2 * block), :] = inter_ref[...].astype(BF16)


def pack(coef, labels, transforms, capacity):
    confs = coef.shape[1]
    rows = 2 * 3 * confs
    return pl.pallas_call(
        functools.partial(pack_kernel, capacity),
        out_shape=(
            jax.ShapeDtypeStruct((rows, 128), BF16),
            jax.ShapeDtypeStruct((1, confs), jnp.int32),
        ),
        scratch_shapes=[pltpu.VMEM((512, 128), F32)],
        compiler_params=pltpu.CompilerParams(vmem_limit_bytes=VMEM_LIMIT),
        name="pack",
    )(coef, labels, transforms)


def build_table(x_ref, table_ref, stage_ref):
    blocks, rows, _ = x_ref.shape
    lanes = rows // 3

    def build(j, carry):
        stage_ref[...] = x_ref[j].astype(F32)
        for ct in range(3):
            piece = stage_ref[pl.ds(ct, lanes, stride=3), :]
            piece = jnp.concatenate([piece, jnp.zeros((128 - lanes, 128), F32)], axis=0)
            start = pl.multiple_of((j * 3 + ct) * 128 + PAD, 8)
            table_ref[pl.ds(start, 128), :] = piece.T
        return carry

    lax.fori_loop(0, blocks, build, 0)


def plan_kernel(steps, tgt_ref, val_ref, cnt_ref, out_ref):
    exc, length = tgt_ref.shape
    counts = cnt_ref[...]
    place = lax.broadcasted_iota(jnp.int32, (1, length), 1)
    key = counts * 4096 + (4095 - place)
    key8 = jnp.broadcast_to(key, (8, length)).astype(F32)
    slots = lax.broadcasted_iota(jnp.int32, (exc, length), 0)
    live = jnp.where(slots < counts, val_ref[...].astype(F32), 0.0)
    tgt = tgt_ref[...]
    high = tgt >> 7
    rows = lax.broadcasted_iota(jnp.int32, (8, length), 0)
    extra = jnp.where(rows == 0, place >> 7, jnp.where(rows == 1, place & 127, 0))
    lists = jnp.concatenate(
        [high.astype(F32), (tgt & 127).astype(F32), live, extra.astype(F32)], axis=0
    ).astype(BF16)
    total = jnp.zeros((lists.shape[0], length), F32)
    for k in range(length // 128):
        mine = key8[:, k * 128 : (k + 1) * 128]
        column = jnp.concatenate([mine] * 16, axis=0).T[:, 0:1]
        ahead = jnp.where(key8[0:1, :] > column, 1.0, 0.0)
        rank = jnp.sum(ahead, axis=1, keepdims=True).astype(jnp.int32)
        moved = (
            (lax.broadcasted_iota(jnp.int32, (128, length), 1) == rank).astype(F32).astype(BF16)
        )
        total = total + jnp.dot(
            lists[:, k * 128 : (k + 1) * 128], moved, preferred_element_type=F32
        )
    lane = lax.broadcasted_iota(jnp.int32, (8, length), 1)
    bounds = jnp.zeros((8, length), F32)
    for k in range(exc // steps):
        over = jnp.sum(jnp.where(counts > k * steps, 1.0, 0.0), axis=1, keepdims=True)
        groups = ((over.astype(jnp.int32) + 7) >> 3).astype(F32)
        bounds = jnp.where(jnp.logical_and(lane == k, rows == 2), groups, bounds)
    out_ref[0 : 3 * exc, :] = total[: 3 * exc]
    out_ref[3 * exc :, :] = jnp.where(rows == 2, bounds, total[3 * exc :])


def plan(targets, values, counts, steps):
    exc, length = targets.shape
    return pl.pallas_call(
        functools.partial(plan_kernel, steps),
        out_shape=jax.ShapeDtypeStruct((3 * exc + 8, length), F32),
        compiler_params=pltpu.CompilerParams(vmem_limit_bytes=VMEM_LIMIT),
        name="plan",
    )(targets, values, counts[None, :])


def beta_block(table_ref, tgt_ref, row_ref, w_ref, out_ref, wt_ref, acc_ref):
    lanes = out_ref.shape[1] // 3
    exc = 16
    cols = 384
    sub = lax.broadcasted_iota(jnp.int32, (8, 128), 0)
    for ct in range(3):
        wt_ref[pl.ds(ct * 128, 128), :] = jnp.concatenate(
            [w_ref[0, pl.ds(ct, exc, stride=3), :], jnp.zeros((128 - exc, 128), F32)], axis=0
        ).T
    buckets = exc // STEPS
    at = (exc + 1) * cols

    def make(depth):
        def group(g, carry):
            first = pl.multiple_of(g * 8, 8)
            near = tgt_ref.at[pl.ds(first, exc * cols)]
            w8 = wt_ref[pl.ds(first, 8), :]
            acc = jnp.zeros((8, 128), F32)
            for e in range(depth):
                got = None
                for s in range(8):
                    t = near[e * cols + s]
                    win = table_ref[pl.ds(t + (PAD - s), 8), :]
                    got = win if s == 0 else jnp.where(sub == s, win, got)
                acc = acc + got * w8[:, e : e + 1]
            acc_ref[pl.ds(first, 8), :] = acc
            return carry

        return group

    for k in reversed(range(buckets)):
        begin = tgt_ref[at + k + 1] if k + 1 < buckets else 0
        lax.fori_loop(begin, tgt_ref[at + k], make((k + 1) * STEPS), 0)
    ids = jnp.concatenate([row_ref[0, exc * 3 + ct : exc * 3 + ct + 1, :] for ct in range(3)], axis=1)
    back = (
        (lax.broadcasted_iota(jnp.int32, (cols, cols), 0) == ids).astype(F32).astype(BF16)
    )
    left = acc_ref[...].T
    done = jnp.zeros((128, cols), F32)
    for part in range(3):
        piece = left.astype(BF16)
        done = done + lax.dot_general(
            piece, back, (((1,), (1,)), ((), ())), preferred_element_type=F32
        )
        left = left - piece.astype(F32)
    for ct in range(3):
        out_ref[0, pl.ds(ct, lanes, stride=3), :] = done[:lanes, ct * 128 : (ct + 1) * 128]


def beta_first_kernel(
    x_ref, tgt_ref, row_ref, w_ref, out_ref, table_ref, wt_ref, acc_ref, stage_ref
):
    @pl.when(pl.program_id(0) == 0)
    def _():
        build_table(x_ref, table_ref, stage_ref)

    beta_block(table_ref, tgt_ref, row_ref, w_ref, out_ref, wt_ref, acc_ref)


def beta_rest_kernel(table_ref, tgt_ref, row_ref, w_ref, out_ref, wt_ref, acc_ref):
    beta_block(table_ref, tgt_ref, row_ref, w_ref, out_ref, wt_ref, acc_ref)


def list_specs(skip):
    return [
        pl.BlockSpec((8192,), lambda j: (j + skip,), memory_space=pltpu.SMEM),
        pl.BlockSpec((1, 64, 128), lambda j: (j + skip, 0, 0)),
        pl.BlockSpec((1, 48, 128), lambda j: (j + skip, 0, 0)),
    ]


def beta_params(blocks):
    return dict(
        compiler_params=pltpu.CompilerParams(
            vmem_limit_bytes=VMEM_LIMIT
        ),
        cost_estimate=pl.CostEstimate(
            flops=blocks * 8 * 10**8, bytes_accessed=blocks * 2**20, transcendentals=0
        ),
    )


def beta_first(x2, numbers, weights, blocks):
    nbeta, rows, _ = x2.shape
    height = nbeta * 384 + 2 * PAD
    return pl.pallas_call(
        beta_first_kernel,
        out_shape=(
            jax.ShapeDtypeStruct((blocks, rows, 128), F32),
            jax.ShapeDtypeStruct((height, 128), F32),
        ),
        grid=(blocks,),
        in_specs=[pl.BlockSpec((nbeta, rows, 128), lambda j: (0, 0, 0))] + list_specs(0),
        out_specs=(
            pl.BlockSpec((1, rows, 128), lambda j: (j, 0, 0)),
            pl.BlockSpec((height, 128), lambda j: (0, 0)),
        ),
        scratch_shapes=[
            pltpu.VMEM((384, 128), F32),
            pltpu.VMEM((384, 128), F32),
            pltpu.VMEM((rows, 128), F32),
        ],
        name="beta_first",
        **beta_params(blocks),
    )(x2, numbers.reshape(-1), numbers, weights)


def beta_rest(table, numbers, weights, rows, skip):
    blocks = numbers.shape[0] - skip
    return pl.pallas_call(
        beta_rest_kernel,
        out_shape=jax.ShapeDtypeStruct((blocks, rows, 128), F32),
        grid=(blocks,),
        in_specs=[pl.BlockSpec(table.shape, lambda j: (0, 0))] + list_specs(skip),
        out_specs=pl.BlockSpec((1, rows, 128), lambda j: (j, 0, 0)),
        scratch_shapes=[pltpu.VMEM((384, 128), F32), pltpu.VMEM((384, 128), F32)],
        name="beta_rest",
        **beta_params(blocks),
    )(table, numbers.reshape(-1), numbers, weights)


def alpha_kernel(
    nalpha,
    nbeta,
    own_ref,
    tbl_hbm,
    tgt_ref,
    w_ref,
    diag_ref,
    order_ref,
    out_ref,
    table_ref,
    plane_ref,
    wt_ref,
    acc_ref,
    buf_ref,
    sem,
):
    chunk = buf_ref.shape[1]
    total = tbl_hbm.shape[0]
    n = total // chunk
    exc = w_ref.shape[0]
    rows = diag_ref.shape[0]
    pheight = rows + PAD

    def fetch(k, slot):
        return pltpu.make_async_copy(
            tbl_hbm.at[pl.ds(pl.multiple_of(k * chunk, 16), chunk), :],
            buf_ref.at[slot],
            sem.at[slot],
        )

    fetch(0, 0).start()
    for ct in range(3):
        plane_ref[pl.ds(ct * pheight, rows), :] = diag_ref[:, ct * 128 : (ct + 1) * 128]
    for k in range(rows // 128):
        wt_ref[pl.ds(k * 128, 128), :] = jnp.concatenate(
            [w_ref[:, k * 128 : (k + 1) * 128], jnp.zeros((128 - exc, 128), F32)], axis=0
        ).T

    def load(k, carry):
        slot = lax.rem(k, 2)

        @pl.when(k + 1 < n)
        def _():
            fetch(k + 1, 1 - slot).start()

        fetch(k, slot).wait()
        table_ref[pl.ds(pl.multiple_of(k * chunk + PAD, 8), chunk), :] = buf_ref[slot].astype(F32)
        return carry

    lax.fori_loop(0, n, load, 0)
    sub = lax.broadcasted_iota(jnp.int32, (8, 128), 0)
    buckets = exc // STEPS
    ids = exc * rows
    at = ids + rows

    def make(depth):
        def group(g, carry):
            first = pl.multiple_of(g * 8, 8)
            near = tgt_ref.at[pl.ds(first, ids + 8)]
            w8 = wt_ref[pl.ds(first, 8), :]
            acc = [jnp.zeros((8, 128), F32)] * 3
            for e in range(depth):
                got = [None] * 3
                for s in range(8):
                    t = near[e * rows + s]
                    for ct in range(3):
                        win = table_ref[pl.ds(t + (ct + PAD - s), 8), :]
                        got[ct] = win if s == 0 else jnp.where(sub == s, win, got[ct])
                w = jnp.broadcast_to(w8[:, e : e + 1], (8, 128))
                for ct in range(3):
                    acc[ct] = acc[ct] + got[ct] * w
            for s in range(8):
                a = near[ids + s]
                for ct in range(3):
                    pltpu.store(
                        acc_ref.at[pl.ds(a + (ct + PAD - s), 8), :], acc[ct], mask=sub == s
                    )
            return carry

        return group

    for k in reversed(range(buckets)):
        begin = tgt_ref[at + k + 1] if k + 1 < buckets else 0
        lax.fori_loop(begin, tgt_ref[at + k], make((k + 1) * STEPS), 0)

    per = rows // (nalpha * nbeta)
    own = own_ref[0]
    lower = sub < 4
    pairs = nalpha // 2

    def couple(m, carry):
        beta_s = m // pairs
        base0 = ((m - beta_s * pairs) * 2 * nbeta + beta_s) * per
        base1 = base0 + nbeta * per
        for g, places in enumerate(((base0,), (base0 + 8, base1 - 4), (base1 + 4,))):
            for ct in range(3):
                values = [
                    acc_ref[pl.ds(p * 3 + (ct + PAD), 8, stride=3), :]
                    + plane_ref[pl.ds(p + ct * pheight, 8), :]
                    * table_ref[pl.ds((own + p) * 3 + (ct + PAD), 8, stride=3), :]
                    for p in places
                ]
                value = values[0] if len(values) == 1 else jnp.where(lower, values[0], values[1])
                out_ref[pl.ds(m * (6 * per) + (g * 24 + ct), 8, stride=3), :] = value
        return carry

    lax.fori_loop(0, pairs * nbeta, couple, 0)


def alpha_term(own, table, numbers, weights, diag, order, nalpha, nbeta):
    rows = diag.shape[0]
    total = table.shape[0]
    chunk = total // 16
    return pl.pallas_call(
        functools.partial(alpha_kernel, nalpha, nbeta),
        out_shape=jax.ShapeDtypeStruct((rows * 3, 128), F32),
        in_specs=[
            pl.BlockSpec(memory_space=pltpu.SMEM),
            pl.BlockSpec(memory_space=pl.ANY),
            pl.BlockSpec(memory_space=pltpu.SMEM),
            pl.BlockSpec(memory_space=pltpu.VMEM),
            pl.BlockSpec(memory_space=pltpu.VMEM),
            pl.BlockSpec(memory_space=pl.ANY),
        ],
        out_specs=pl.BlockSpec(memory_space=pltpu.VMEM),
        scratch_shapes=[
            pltpu.VMEM((total + 4 * PAD, 128), F32),
            pltpu.VMEM((rows * 3 + 3 * PAD, 128), F32),
            pltpu.VMEM((rows, 128), F32),
            pltpu.VMEM((rows * 3 + 4 * PAD, 128), F32),
            pltpu.VMEM((2, chunk, 128), BF16),
            pltpu.SemaphoreType.DMA((2,)),
        ],
        compiler_params=pltpu.CompilerParams(
            vmem_limit_bytes=VMEM_LIMIT
        ),
        cost_estimate=pl.CostEstimate(
            flops=10**10, bytes_accessed=16 * 2**20, transcendentals=0
        ),
        name="alpha_term",
    )(own, table, numbers, weights, diag, order)


def unpack_kernel(
    r_ref, key_ref, label_ref, coef_ref, tr_ref, sigma_ref, part_ref, stage_ref, half_ref
):
    rows2 = r_ref.shape[0]
    rows = rows2 // 2
    confs = key_ref.shape[1]
    width = coef_ref.shape[0]
    ncls = tr_ref.shape[0]
    tall = width + -width % 8
    stage_ref[...] = r_ref[...].astype(F32)
    for h in range(2):
        half_ref[:, h * 128 : (h + 1) * 128] = stage_ref[pl.ds(h, rows, stride=2), :].astype(BF16)
    key = key_ref[...]
    block = 256
    dets = jnp.zeros((256, confs), F32)
    for b in range(rows // block):
        onehot = (
            (lax.broadcasted_iota(jnp.int32, (block, confs), 0) + b * block == key)
            .astype(F32)
            .astype(BF16)
        )
        dets = dets + lax.dot_general(
            half_ref[pl.ds(b * block, block), :],
            onehot,
            (((0,), (0,)), ((), ())),
            preferred_element_type=F32,
        )
    trans = jnp.concatenate([padded(tr_ref, c) for c in range(ncls)], axis=0)
    products = jnp.dot(trans, dets, precision=HIGH, preferred_element_type=F32)
    sigma = jnp.zeros((width, confs), F32)
    for c in range(ncls):
        part = products[c * tall : c * tall + width]
        sigma = sigma + jnp.where(label_ref[0:1, :] == c, part, 0.0)
    coef = coef_ref[...]
    sigma_ref[...] = sigma
    square = jnp.sum(jnp.sum(coef * coef, axis=1, keepdims=True), axis=0, keepdims=True)
    cross = jnp.sum(jnp.sum(coef * sigma, axis=1, keepdims=True), axis=0, keepdims=True)
    ratio = jnp.where(square > 0.0, cross / jnp.where(square > 0.0, square, 1.0), 0.0)
    rest = sigma - ratio * coef
    rho = jnp.sum(jnp.sum(rest * rest, axis=1, keepdims=True), axis=0, keepdims=True)
    lane = lax.broadcasted_iota(jnp.int32, (1, 128), 1)
    part_ref[...] = jnp.where(
        lane == 0,
        square,
        jnp.where(lane == 1, cross, jnp.where(lane == 2, rho, jnp.where(lane == 3, ratio, 0.0))),
    )


def unpack(returned, key, labels, coef, transforms):
    return pl.pallas_call(
        unpack_kernel,
        out_shape=(
            jax.ShapeDtypeStruct(coef.shape, F32),
            jax.ShapeDtypeStruct((1, 128), F32),
        ),
        scratch_shapes=[
            pltpu.VMEM(returned.shape, F32),
            pltpu.VMEM((returned.shape[0] // 2, 256), BF16),
        ],
        compiler_params=pltpu.CompilerParams(vmem_limit_bytes=VMEM_LIMIT),
        name="unpack",
    )(returned, key, labels, coef, transforms)


def exchange(x, axes):
    return lax.all_to_all(x, axes, split_axis=0, concat_axis=0, tiled=True)


def body(
    csf_coef,
    conf_class,
    conf_tile,
    transforms,
    alpha_targets,
    alpha_values,
    alpha_counts,
    beta_targets,
    beta_values,
    beta_counts,
    det_diag,
):
    nalpha = lax.axis_size("alpha")
    nbeta = lax.axis_size("beta")
    devices = nalpha * nbeta
    ncsf, confs = csf_coef.shape
    capacity = 3 * confs // devices
    rows_alpha = det_diag.shape[0]
    width = transforms.shape[2]
    exc = alpha_targets.shape[0]
    pieces = capacity * width // 128
    labels = jnp.stack([conf_class, conf_tile[:, 0]])
    bplan = plan(beta_targets, beta_values, beta_counts, STEPS)
    zero = jnp.zeros((1, bplan.shape[1]), F32)
    lists = jnp.concatenate(
        [
            bplan[:exc],
            bplan[3 * exc : 3 * exc + 1],
            zero,
            bplan[exc : 2 * exc],
            bplan[3 * exc + 1 : 3 * exc + 3],
            bplan[2 * exc : 3 * exc],
        ],
        axis=0,
    ).astype(BF16)
    lists = lists.reshape(-1, 128)
    lists = jnp.pad(lists, ((0, -lists.shape[0] % 16), (0, 0)))
    aplan = plan(alpha_targets, alpha_values, alpha_counts, STEPS)
    anumbers = jnp.concatenate(
        [
            aplan[:exc] * 384.0 + aplan[exc : 2 * exc] * 3.0,
            aplan[3 * exc : 3 * exc + 1] * 384.0 + aplan[3 * exc + 1 : 3 * exc + 2] * 3.0,
            aplan[3 * exc + 2 : 3 * exc + 3],
        ],
        axis=0,
    )
    anumbers = anumbers.astype(jnp.int32).reshape(-1)
    aweights = aplan[2 * exc : 3 * exc]

    outgoing, key = pack(csf_coef, labels, transforms, capacity)
    tile = exchange(outgoing.reshape(devices, pieces, 128), BOTH)
    flat = tile.reshape(-1, 128)
    table = lax.all_gather(flat, "alpha", axis=0, tiled=True)

    body_rows = nalpha * pieces
    spread = (
        tile.reshape(nalpha, nbeta, pieces, 128)
        .transpose(1, 0, 2, 3)
        .reshape(nbeta, body_rows, 128)
    )
    sent = jnp.concatenate(
        [spread, jnp.broadcast_to(lists[None], (nbeta,) + lists.shape)], axis=1
    )
    got = exchange(sent, "beta")
    x2 = got[:, :body_rows]
    nrows = (exc + 2) * (bplan.shape[1] // 128)
    wrows = exc * (bplan.shape[1] // 128)
    high = got[:, body_rows : body_rows + nrows].astype(jnp.int32)
    low = got[:, body_rows + nrows : body_rows + 2 * nrows].astype(jnp.int32)
    bnumbers = jnp.pad(high * 128 + low, ((0, 0), (0, 64 - nrows), (0, 0)))
    bweights = got[:, body_rows + 2 * nrows : body_rows + 2 * nrows + wrows].astype(F32)

    beta_a, btable = beta_first(x2, bnumbers, bweights, FIRST)
    own = (lax.axis_index("alpha") * rows_alpha).astype(jnp.int32)[None]
    partial = alpha_term(own, table, anumbers, aweights, det_diag, beta_a, nalpha, nbeta)
    passed = exchange(partial.reshape(nbeta, body_rows, 128), "beta")
    beta_b = beta_rest(btable, bnumbers, bweights, body_rows, FIRST)
    sigma_slab = (
        (passed + jnp.concatenate([beta_a, beta_b], axis=0))
        .astype(BF16)
        .reshape(nbeta, nalpha, pieces, 128)
        .transpose(1, 0, 2, 3)
        .reshape(nalpha, nbeta * pieces, 128)
    )
    returned = exchange(sigma_slab, "alpha").reshape(-1, 128)
    sigma, part = unpack(returned, key, labels, csf_coef, transforms)
    parts = exchange(jnp.broadcast_to(part[None], (devices, 1, 128)), BOTH)[:, 0]
    square = parts[:, 0]
    rayleigh = jnp.sum(parts[:, 1]) / jnp.sum(square)
    shift = rayleigh - parts[:, 3]
    residual_square = jnp.sum(parts[:, 2] + shift * shift * square)
    residual = sigma - rayleigh * csf_coef
    residual_rms = jnp.sqrt(residual_square / (ncsf * confs * devices))
    return (residual, residual_rms)


def solution(mesh):
    placed = (
        P(None, BOTH),
        P(BOTH),
        P(BOTH, None),
        P(),
        P(None, "alpha"),
        P(None, "alpha"),
        P("alpha"),
        P(None, "beta"),
        P(None, "beta"),
        P("beta"),
        P("alpha", "beta"),
    )
    return jax.shard_map(
        body,
        mesh=mesh,
        in_specs=placed,
        out_specs=(P(None, BOTH), P()),
        check_vma=False,
    )
```

```python
import functools

import jax
import jax.numpy as jnp
from jax import lax
from jax.experimental import pallas as pl
from jax.experimental.pallas import tpu as pltpu
from jax.sharding import PartitionSpec as P


F32 = jnp.float32
BF16 = jnp.bfloat16
HIGH = lax.Precision.HIGHEST
BOTH = ("alpha", "beta")
PAD = 8
FIRST = 4
STEPS = 2
VMEM_LIMIT = 60 * 1024 * 1024


def stacked(coef, classes, classes_n):
    parts = []
    for c in range(classes_n):
        parts.append(jnp.where(classes == c, coef, jnp.zeros_like(coef)))
    return jnp.concatenate(parts, axis=0)


def padded(ref, index=None):
    value = ref[...] if index is None else ref[index]
    fill = -value.shape[0] % 8
    return jnp.concatenate([value, jnp.zeros((fill, value.shape[1]), F32)], axis=0)


def pack_kernel(capacity, coef_ref, label_ref, tr_ref, out_ref, key_ref, inter_ref):
    confs = coef_ref.shape[1]
    ncls = tr_ref.shape[0]
    devices = confs * 3 // capacity
    masked = stacked(padded(coef_ref), label_ref[0:1, :], ncls)
    trans = jnp.concatenate([padded(tr_ref, c) for c in range(ncls)], axis=0)
    dets = lax.dot_general(
        masked, trans, (((0,), (0,)), ((), ())), precision=HIGH, preferred_element_type=F32
    ).astype(BF16)
    tile = label_ref[1:2, :]
    hit = lax.broadcasted_iota(jnp.int32, (devices, confs), 0) == tile
    before = lax.broadcasted_iota(jnp.int32, (confs, confs), 0) < lax.broadcasted_iota(
        jnp.int32, (confs, confs), 1
    )
    counts = jnp.dot(
        hit.astype(F32).astype(BF16), before.astype(F32).astype(BF16), preferred_element_type=F32
    )
    slot = jnp.sum(jnp.where(hit, counts, 0.0), axis=0, keepdims=True).astype(jnp.int32)
    key = tile * capacity + slot
    key_ref[...] = key
    rows = devices * capacity
    block = 256
    for b in range(rows // block):
        onehot = (
            (lax.broadcasted_iota(jnp.int32, (block, confs), 0) + b * block == key)
            .astype(F32)
            .astype(BF16)
        )
        picked = jnp.dot(onehot, dets, preferred_element_type=F32)
        for h in range(2):
            inter_ref[pl.ds(h, block, stride=2), :] = picked[:, h * 128 : (h + 1) * 128]
        out_ref[pl.ds(b * 2 * block, 2 * block), :] = inter_ref[...].astype(BF16)


def pack(coef, labels, transforms, capacity):
    confs = coef.shape[1]
    rows = 2 * 3 * confs
    return pl.pallas_call(
        functools.partial(pack_kernel, capacity),
        out_shape=(
            jax.ShapeDtypeStruct((rows, 128), BF16),
            jax.ShapeDtypeStruct((1, confs), jnp.int32),
        ),
        scratch_shapes=[pltpu.VMEM((512, 128), F32)],
        compiler_params=pltpu.CompilerParams(vmem_limit_bytes=VMEM_LIMIT),
        name="pack",
    )(coef, labels, transforms)


def build_table(x_ref, table_ref, stage_ref):
    blocks, rows, _ = x_ref.shape
    lanes = rows // 3

    def build(j, carry):
        stage_ref[...] = x_ref[j].astype(F32)
        for ct in range(3):
            piece = stage_ref[pl.ds(ct, lanes, stride=3), :]
            piece = jnp.concatenate([piece, jnp.zeros((128 - lanes, 128), F32)], axis=0)
            start = pl.multiple_of((j * 3 + ct) * 128 + PAD, 8)
            table_ref[pl.ds(start, 128), :] = piece.T
        return carry

    lax.fori_loop(0, blocks, build, 0)


def plan_kernel(steps, tgt_ref, val_ref, cnt_ref, out_ref):
    exc, length = tgt_ref.shape
    counts = cnt_ref[...]
    place = lax.broadcasted_iota(jnp.int32, (1, length), 1)
    key = counts * 4096 + (4095 - place)
    key8 = jnp.broadcast_to(key, (8, length)).astype(F32)
    slots = lax.broadcasted_iota(jnp.int32, (exc, length), 0)
    live = jnp.where(slots < counts, val_ref[...].astype(F32), 0.0)
    tgt = tgt_ref[...]
    high = tgt >> 7
    rows = lax.broadcasted_iota(jnp.int32, (8, length), 0)
    extra = jnp.where(rows == 0, place >> 7, jnp.where(rows == 1, place & 127, 0))
    lists = jnp.concatenate(
        [high.astype(F32), (tgt & 127).astype(F32), live, extra.astype(F32)], axis=0
    ).astype(BF16)
    total = jnp.zeros((lists.shape[0], length), F32)
    for k in range(length // 128):
        mine = key8[:, k * 128 : (k + 1) * 128]
        column = jnp.concatenate([mine] * 16, axis=0).T[:, 0:1]
        ahead = jnp.where(key8[0:1, :] > column, 1.0, 0.0)
        rank = jnp.sum(ahead, axis=1, keepdims=True).astype(jnp.int32)
        moved = (
            (lax.broadcasted_iota(jnp.int32, (128, length), 1) == rank).astype(F32).astype(BF16)
        )
        total = total + jnp.dot(
            lists[:, k * 128 : (k + 1) * 128], moved, preferred_element_type=F32
        )
    lane = lax.broadcasted_iota(jnp.int32, (8, length), 1)
    bounds = jnp.zeros((8, length), F32)
    for k in range(exc // steps):
        over = jnp.sum(jnp.where(counts > k * steps, 1.0, 0.0), axis=1, keepdims=True)
        groups = ((over.astype(jnp.int32) + 7) >> 3).astype(F32)
        bounds = jnp.where(jnp.logical_and(lane == k, rows == 2), groups, bounds)
    out_ref[0 : 3 * exc, :] = total[: 3 * exc]
    out_ref[3 * exc :, :] = jnp.where(rows == 2, bounds, total[3 * exc :])


def plan(targets, values, counts, steps):
    exc, length = targets.shape
    return pl.pallas_call(
        functools.partial(plan_kernel, steps),
        out_shape=jax.ShapeDtypeStruct((3 * exc + 8, length), F32),
        compiler_params=pltpu.CompilerParams(vmem_limit_bytes=VMEM_LIMIT),
        name="plan",
    )(targets, values, counts[None, :])


def beta_block(table_ref, tgt_ref, row_ref, w_ref, out_ref, wt_ref, acc_ref):
    lanes = out_ref.shape[1] // 3
    exc = 16
    cols = 384
    sub = lax.broadcasted_iota(jnp.int32, (8, 128), 0)
    for ct in range(3):
        wt_ref[pl.ds(ct * 128, 128), :] = jnp.concatenate(
            [w_ref[0, pl.ds(ct, exc, stride=3), :], jnp.zeros((128 - exc, 128), F32)], axis=0
        ).T
    buckets = exc // STEPS
    at = (exc + 1) * cols

    def make(depth):
        def group(g, carry):
            first = pl.multiple_of(g * 8, 8)
            near = tgt_ref.at[pl.ds(first, exc * cols)]
            w8 = wt_ref[pl.ds(first, 8), :]
            acc = jnp.zeros((8, 128), F32)
            for e in range(depth):
                got = None
                for s in range(8):
                    t = near[e * cols + s]
                    win = table_ref[pl.ds(t + (PAD - s), 8), :]
                    got = win if s == 0 else jnp.where(sub == s, win, got)
                acc = acc + got * w8[:, e : e + 1]
            acc_ref[pl.ds(first, 8), :] = acc
            return carry

        return group

    for k in reversed(range(buckets)):
        begin = tgt_ref[at + k + 1] if k + 1 < buckets else 0
        lax.fori_loop(begin, tgt_ref[at + k], make((k + 1) * STEPS), 0)
    ids = jnp.concatenate([row_ref[0, exc * 3 + ct : exc * 3 + ct + 1, :] for ct in range(3)], axis=1)
    back = (
        (lax.broadcasted_iota(jnp.int32, (cols, cols), 0) == ids).astype(F32).astype(BF16)
    )
    left = acc_ref[...].T
    done = jnp.zeros((128, cols), F32)
    for _ in range(3):
        piece = left.astype(BF16)
        done = done + lax.dot_general(
            piece, back, (((1,), (1,)), ((), ())), preferred_element_type=F32
        )
        left = left - piece.astype(F32)
    for ct in range(3):
        out_ref[0, pl.ds(ct, lanes, stride=3), :] = done[:lanes, ct * 128 : (ct + 1) * 128]


def beta_first_kernel(
    x_ref, tgt_ref, row_ref, w_ref, out_ref, table_ref, wt_ref, acc_ref, stage_ref
):
    @pl.when(pl.program_id(0) == 0)
    def _():
        build_table(x_ref, table_ref, stage_ref)

    beta_block(table_ref, tgt_ref, row_ref, w_ref, out_ref, wt_ref, acc_ref)


def beta_rest_kernel(table_ref, tgt_ref, row_ref, w_ref, old_ref, out_ref, wt_ref, acc_ref):
    beta_block(table_ref, tgt_ref, row_ref, w_ref, out_ref, wt_ref, acc_ref)


def list_specs(skip):
    return [
        pl.BlockSpec((8192,), lambda j: (j + skip,), memory_space=pltpu.SMEM),
        pl.BlockSpec((1, 64, 128), lambda j: (j + skip, 0, 0)),
        pl.BlockSpec((1, 48, 128), lambda j: (j + skip, 0, 0)),
    ]


def beta_params(blocks):
    return dict(
        compiler_params=pltpu.CompilerParams(vmem_limit_bytes=VMEM_LIMIT),
        cost_estimate=pl.CostEstimate(
            flops=blocks * 8 * 10**8, bytes_accessed=blocks * 2**20, transcendentals=0
        ),
    )


def beta_first(x2, numbers, weights, blocks):
    nbeta, rows, _ = x2.shape
    height = nbeta * 384 + 2 * PAD
    return pl.pallas_call(
        beta_first_kernel,
        out_shape=(
            jax.ShapeDtypeStruct((nbeta, rows, 128), F32),
            jax.ShapeDtypeStruct((height, 128), F32),
        ),
        grid=(blocks,),
        in_specs=[pl.BlockSpec((nbeta, rows, 128), lambda j: (0, 0, 0))] + list_specs(0),
        out_specs=(
            pl.BlockSpec((1, rows, 128), lambda j: (j, 0, 0)),
            pl.BlockSpec((height, 128), lambda j: (0, 0)),
        ),
        scratch_shapes=[
            pltpu.VMEM((384, 128), F32),
            pltpu.VMEM((384, 128), F32),
            pltpu.VMEM((rows, 128), F32),
        ],
        name="beta_first",
        **beta_params(blocks),
    )(x2, numbers.reshape(-1), numbers, weights)


def beta_rest(table, numbers, weights, partial, skip):
    nbeta, rows, _ = partial.shape
    return pl.pallas_call(
        beta_rest_kernel,
        out_shape=jax.ShapeDtypeStruct(partial.shape, F32),
        grid=(nbeta - skip,),
        in_specs=[pl.BlockSpec(table.shape, lambda j: (0, 0))]
        + list_specs(skip)
        + [pl.BlockSpec(memory_space=pl.ANY)],
        out_specs=pl.BlockSpec((1, rows, 128), lambda j: (j + skip, 0, 0)),
        scratch_shapes=[pltpu.VMEM((384, 128), F32), pltpu.VMEM((384, 128), F32)],
        input_output_aliases={4: 0},
        name="beta_rest",
        **beta_params(nbeta - skip),
    )(table, numbers.reshape(-1), numbers, weights, partial)


def alpha_kernel(
    own_ref,
    tbl_hbm,
    tgt_ref,
    w_ref,
    diag_ref,
    order_ref,
    out_ref,
    table_ref,
    wt_ref,
    acc_ref,
    buf_ref,
    sem,
):
    chunk = buf_ref.shape[1]
    total = tbl_hbm.shape[0]
    n = total // chunk
    exc = w_ref.shape[0]
    rows = diag_ref.shape[0]

    def fetch(k):
        return pltpu.make_async_copy(
            tbl_hbm.at[pl.ds(k * chunk, chunk), :], buf_ref.at[k], sem.at[k]
        )

    for k in range(n):
        fetch(k).start()
    for k in range(rows // 128):
        turned = jnp.concatenate(
            [w_ref[:, k * 128 : (k + 1) * 128], jnp.zeros((128 - exc, 128), F32)], axis=0
        ).T
        for ct in range(3):
            wt_ref[pl.ds(k * 384 + ct, 128, stride=3), :] = turned

    for k in range(n):
        fetch(k).wait()

        def widen(i, carry):
            start = pl.multiple_of(i * 128, 128)
            table_ref[pl.ds(pl.multiple_of(start + (k * chunk + PAD), 8), 128), :] = buf_ref[
                k, pl.ds(start, 128), :
            ].astype(F32)
            return carry

        lax.fori_loop(0, chunk // 128, widen, 0)
    sub = lax.broadcasted_iota(jnp.int32, (8, 128), 0)
    buckets = exc // STEPS
    ids = exc * rows
    at = ids + rows

    front = sub < 3
    back = jnp.logical_and(sub >= 3, sub < 6)

    def make(depth):
        def group(g, carry):
            first = pl.multiple_of(g * 8, 8)
            near = tgt_ref.at[pl.ds(first, ids + 8)]
            w6 = [wt_ref[pl.ds(first * 3 + 6 * q, 8), :] for q in range(4)]
            acc = [jnp.zeros((8, 128), F32)] * 4
            for e in range(depth):
                for q in range(4):
                    low = table_ref[pl.ds(near[e * rows + 2 * q] + PAD, 8), :]
                    high = table_ref[pl.ds(near[e * rows + 2 * q + 1] + (PAD - 3), 8), :]
                    w = jnp.broadcast_to(w6[q][:, e : e + 1], (8, 128))
                    acc[q] = acc[q] + jnp.where(front, low, high) * w
            for q in range(4):
                low = near[ids + 2 * q] + PAD
                high = near[ids + 2 * q + 1] + (PAD - 3)
                pltpu.store(acc_ref.at[pl.ds(low, 8), :], acc[q], mask=front)
                pltpu.store(acc_ref.at[pl.ds(high, 8), :], acc[q], mask=back)
            return carry

        return group

    for k in reversed(range(buckets)):
        begin = tgt_ref[at + k + 1] if k + 1 < buckets else 0
        lax.fori_loop(begin, tgt_ref[at + k], make((k + 1) * STEPS), 0)

    own = own_ref[0]

    def finish(i, carry):
        for u in range(4):
            place = pl.multiple_of(i * 32 + u * 8, 8)
            for ct in range(3):
                spot = place * 3 + (ct + PAD)
                out_ref[pl.ds(place * 3 + ct, 8, stride=3), :] = (
                    acc_ref[pl.ds(spot, 8, stride=3), :]
                    + diag_ref[pl.ds(place, 8), ct * 128 : (ct + 1) * 128]
                    * table_ref[pl.ds(own * 3 + spot, 8, stride=3), :]
                )
        return carry

    lax.fori_loop(0, rows // 32, finish, 0)


def alpha_term(own, table, numbers, weights, diag, order):
    rows = diag.shape[0]
    total = table.shape[0]
    chunk = total // 8
    return pl.pallas_call(
        alpha_kernel,
        out_shape=jax.ShapeDtypeStruct((rows * 3, 128), F32),
        in_specs=[
            pl.BlockSpec(memory_space=pltpu.SMEM),
            pl.BlockSpec(memory_space=pl.ANY),
            pl.BlockSpec(memory_space=pltpu.SMEM),
            pl.BlockSpec(memory_space=pltpu.VMEM),
            pl.BlockSpec(memory_space=pltpu.VMEM),
            pl.BlockSpec(memory_space=pl.ANY),
        ],
        out_specs=pl.BlockSpec(memory_space=pltpu.VMEM),
        scratch_shapes=[
            pltpu.VMEM((total + 4 * PAD, 128), F32),
            pltpu.VMEM((rows * 3 + PAD, 128), F32),
            pltpu.VMEM((rows * 3 + 4 * PAD, 128), F32),
            pltpu.VMEM((8, chunk, 128), BF16),
            pltpu.SemaphoreType.DMA((8,)),
        ],
        compiler_params=pltpu.CompilerParams(vmem_limit_bytes=VMEM_LIMIT),
        cost_estimate=pl.CostEstimate(
            flops=10**10, bytes_accessed=16 * 2**20, transcendentals=0
        ),
        name="alpha_term",
    )(own, table, numbers, weights, diag, order)


def merge_kernel(nalpha, alpha_ref, beta_ref, out_ref):
    nbeta = beta_ref.shape[0]
    pieces = out_ref.shape[1]

    def senders(beta_s, carry):
        for alpha_s in range(nalpha):
            p = alpha_s * nbeta + beta_s
            one = alpha_ref[pl.ds(p * pieces, pieces), :]
            other = beta_ref[beta_s, alpha_s * pieces : (alpha_s + 1) * pieces, :]
            out_ref[p] = (one + other).astype(BF16)
        return carry

    lax.fori_loop(0, nbeta, senders, 0)


def merge(alpha, beta, nalpha, pieces):
    devices = nalpha * beta.shape[0]
    return pl.pallas_call(
        functools.partial(merge_kernel, nalpha),
        out_shape=jax.ShapeDtypeStruct((devices, pieces, 128), BF16),
        compiler_params=pltpu.CompilerParams(vmem_limit_bytes=VMEM_LIMIT),
        name="merge",
    )(alpha, beta)


def finish_kernel(entries, parts_ref, sigma_ref, coef_ref, out_ref, rms_ref):
    parts = parts_ref[:, 0, :]
    square = parts[:, 0:1]
    total = jnp.sum(parts, axis=0, keepdims=True)
    rayleigh = total[:, 1:2] / total[:, 0:1]
    shift = rayleigh - parts[:, 3:4]
    rest = jnp.sum(parts[:, 2:3] + shift * shift * square, axis=0, keepdims=True)
    out_ref[...] = sigma_ref[...] - rayleigh * coef_ref[...]
    rms_ref[...] = jnp.sqrt(rest / entries)


def finish(parts, sigma, coef, entries):
    return pl.pallas_call(
        functools.partial(finish_kernel, float(entries)),
        out_shape=(
            jax.ShapeDtypeStruct(sigma.shape, F32),
            jax.ShapeDtypeStruct((1, 1), F32),
        ),
        name="finish",
    )(parts, sigma, coef)


def unpack_kernel(
    r_ref, key_ref, label_ref, coef_ref, tr_ref, sigma_ref, part_ref, stage_ref, half_ref
):
    devices, pieces, _ = r_ref.shape
    rows = devices * pieces // 2
    confs = key_ref.shape[1]
    width = coef_ref.shape[0]
    ncls = tr_ref.shape[0]
    tall = width + -width % 8

    def spread(p, carry):
        stage_ref[pl.ds(p * pieces, pieces), :] = r_ref[p].astype(F32)
        return carry

    lax.fori_loop(0, devices, spread, 0)
    for h in range(2):
        half_ref[:, h * 128 : (h + 1) * 128] = stage_ref[pl.ds(h, rows, stride=2), :].astype(BF16)
    key = key_ref[...]
    block = 256
    dets = jnp.zeros((256, confs), F32)
    for b in range(rows // block):
        onehot = (
            (lax.broadcasted_iota(jnp.int32, (block, confs), 0) + b * block == key)
            .astype(F32)
            .astype(BF16)
        )
        dets = dets + lax.dot_general(
            half_ref[pl.ds(b * block, block), :],
            onehot,
            (((0,), (0,)), ((), ())),
            preferred_element_type=F32,
        )
    trans = jnp.concatenate([padded(tr_ref, c) for c in range(ncls)], axis=0)
    products = jnp.dot(trans, dets, precision=HIGH, preferred_element_type=F32)
    sigma = jnp.zeros((width, confs), F32)
    for c in range(ncls):
        part = products[c * tall : c * tall + width]
        sigma = sigma + jnp.where(label_ref[0:1, :] == c, part, 0.0)
    coef = coef_ref[...]
    sigma_ref[...] = sigma
    square = jnp.sum(jnp.sum(coef * coef, axis=1, keepdims=True), axis=0, keepdims=True)
    cross = jnp.sum(jnp.sum(coef * sigma, axis=1, keepdims=True), axis=0, keepdims=True)
    ratio = jnp.where(square > 0.0, cross / jnp.where(square > 0.0, square, 1.0), 0.0)
    rest = sigma - ratio * coef
    rho = jnp.sum(jnp.sum(rest * rest, axis=1, keepdims=True), axis=0, keepdims=True)
    lane = lax.broadcasted_iota(jnp.int32, (1, 128), 1)
    part_ref[...] = jnp.where(
        lane == 0,
        square,
        jnp.where(lane == 1, cross, jnp.where(lane == 2, rho, jnp.where(lane == 3, ratio, 0.0))),
    )


def unpack(returned, key, labels, coef, transforms):
    return pl.pallas_call(
        unpack_kernel,
        out_shape=(
            jax.ShapeDtypeStruct(coef.shape, F32),
            jax.ShapeDtypeStruct((1, 128), F32),
        ),
        scratch_shapes=[
            pltpu.VMEM((returned.shape[0] * returned.shape[1], 128), F32),
            pltpu.VMEM((returned.shape[0] * returned.shape[1] // 2, 256), BF16),
        ],
        compiler_params=pltpu.CompilerParams(vmem_limit_bytes=VMEM_LIMIT),
        name="unpack",
    )(returned, key, labels, coef, transforms)


def exchange(x, axes):
    return lax.all_to_all(x, axes, split_axis=0, concat_axis=0, tiled=True)


def body(
    csf_coef,
    conf_class,
    conf_tile,
    transforms,
    alpha_targets,
    alpha_values,
    alpha_counts,
    beta_targets,
    beta_values,
    beta_counts,
    det_diag,
):
    nalpha = lax.axis_size("alpha")
    nbeta = lax.axis_size("beta")
    devices = nalpha * nbeta
    ncsf, confs = csf_coef.shape
    capacity = 3 * confs // devices
    rows_alpha = det_diag.shape[0]
    width = transforms.shape[2]
    exc = alpha_targets.shape[0]
    pieces = capacity * width // 128
    labels = jnp.stack([conf_class, conf_tile[:, 0]])
    bplan = plan(beta_targets, beta_values, beta_counts, STEPS)
    zero = jnp.zeros((1, bplan.shape[1]), F32)
    lists = jnp.concatenate(
        [
            bplan[:exc],
            bplan[3 * exc : 3 * exc + 1],
            zero,
            bplan[exc : 2 * exc],
            bplan[3 * exc + 1 : 3 * exc + 3],
            bplan[2 * exc : 3 * exc],
        ],
        axis=0,
    ).astype(BF16)
    lists = lists.reshape(-1, 128)
    lists = jnp.pad(lists, ((0, -lists.shape[0] % 16), (0, 0)))
    aplan = plan(alpha_targets, alpha_values, alpha_counts, STEPS)
    anumbers = jnp.concatenate(
        [
            aplan[:exc] * 384.0 + aplan[exc : 2 * exc] * 3.0,
            aplan[3 * exc : 3 * exc + 1] * 384.0 + aplan[3 * exc + 1 : 3 * exc + 2] * 3.0,
            aplan[3 * exc + 2 : 3 * exc + 3],
        ],
        axis=0,
    )
    anumbers = anumbers.astype(jnp.int32).reshape(-1)
    aweights = aplan[2 * exc : 3 * exc]

    body_rows = nalpha * pieces
    heard = exchange(jnp.broadcast_to(lists[None], (nbeta,) + lists.shape), "beta")
    labels, lists = lax.optimization_barrier((labels, lists))
    outgoing, key = pack(csf_coef, labels, transforms, capacity)
    outgoing, heard = lax.optimization_barrier((outgoing, heard))
    slab = exchange(outgoing.reshape(nalpha, nbeta * pieces, 128), "alpha")
    slab, anumbers, aweights = lax.optimization_barrier((slab, anumbers, aweights))
    x2 = (
        slab.reshape(nalpha, nbeta, pieces, 128)
        .transpose(1, 0, 2, 3)
        .reshape(nbeta, body_rows, 128)
    )
    nrows = (exc + 2) * (bplan.shape[1] // 128)
    wrows = exc * (bplan.shape[1] // 128)
    high = heard[:, :nrows].astype(jnp.int32)
    low = heard[:, nrows : 2 * nrows].astype(jnp.int32)
    bnumbers = jnp.pad(high * 128 + low, ((0, 0), (0, 64 - nrows), (0, 0)))
    bweights = heard[:, 2 * nrows : 2 * nrows + wrows].astype(F32)

    got = exchange(x2, "beta")
    beta_a, btable = beta_first(x2, bnumbers, bweights, FIRST)
    got, btable = lax.optimization_barrier((got, btable))
    flat = (
        got.reshape(nbeta, nalpha, pieces, 128).transpose(1, 0, 2, 3).reshape(-1, 128)
    )
    table = lax.all_gather(flat, "alpha", axis=0, tiled=True)
    beta_b = beta_rest(btable, bnumbers, bweights, beta_a, FIRST)
    beta_tile = exchange(beta_b, "beta")
    own = (lax.axis_index("alpha") * rows_alpha).astype(jnp.int32)[None]
    partial = alpha_term(own, table, anumbers, aweights, det_diag, beta_b)
    sigma_tile = merge(partial, beta_tile, nalpha, pieces)
    returned = exchange(sigma_tile, BOTH)
    sigma, part = unpack(returned, key, labels, csf_coef, transforms)
    parts = exchange(jnp.broadcast_to(part[None], (devices, 1, 128)), BOTH)
    residual, rms = finish(parts, sigma, csf_coef, ncsf * confs * devices)
    return (residual, rms[0, 0])


def solution(mesh):
    placed = (
        P(None, BOTH),
        P(BOTH),
        P(BOTH, None),
        P(),
        P(None, "alpha"),
        P(None, "alpha"),
        P("alpha"),
        P(None, "beta"),
        P(None, "beta"),
        P("beta"),
        P("alpha", "beta"),
    )
    return jax.shard_map(
        body,
        mesh=mesh,
        in_specs=placed,
        out_specs=(P(None, BOTH), P()),
        check_vma=False,
    )
```

```python
import functools

import jax
import jax.numpy as jnp
from jax import lax
from jax.experimental import pallas as pl
from jax.experimental.pallas import tpu as pltpu
from jax.sharding import PartitionSpec as P


F32 = jnp.float32
BF16 = jnp.bfloat16
HIGH = lax.Precision.HIGHEST
BOTH = ("alpha", "beta")
PAD = 8
FIRST = 2
STEPS = 2
WIDE = 32
FEW = 16
VMEM_LIMIT = 60 * 1024 * 1024


def stacked(coef, classes, classes_n):
    parts = []
    for c in range(classes_n):
        parts.append(jnp.where(classes == c, coef, jnp.zeros_like(coef)))
    return jnp.concatenate(parts, axis=0)


def padded(ref, index=None):
    value = ref[...] if index is None else ref[index]
    fill = -value.shape[0] % 8
    return jnp.concatenate([value, jnp.zeros((fill, value.shape[1]), F32)], axis=0)


def pack_kernel(capacity, coef_ref, label_ref, tr_ref, out_ref, key_ref, inter_ref):
    confs = coef_ref.shape[1]
    ncls = tr_ref.shape[0]
    devices = confs * 3 // capacity
    masked = stacked(padded(coef_ref), label_ref[0:1, :], ncls)
    trans = jnp.concatenate([padded(tr_ref, c) for c in range(ncls)], axis=0)
    dets = lax.dot_general(
        masked, trans, (((0,), (0,)), ((), ())), precision=HIGH, preferred_element_type=F32
    ).astype(BF16)
    tile = label_ref[1:2, :]
    hit = lax.broadcasted_iota(jnp.int32, (devices, confs), 0) == tile
    before = lax.broadcasted_iota(jnp.int32, (confs, confs), 0) < lax.broadcasted_iota(
        jnp.int32, (confs, confs), 1
    )
    counts = jnp.dot(
        hit.astype(F32).astype(BF16), before.astype(F32).astype(BF16), preferred_element_type=F32
    )
    slot = jnp.sum(jnp.where(hit, counts, 0.0), axis=0, keepdims=True).astype(jnp.int32)
    key = tile * capacity + slot
    key_ref[...] = key
    rows = devices * capacity
    block = 256
    for b in range(rows // block):
        onehot = (
            (lax.broadcasted_iota(jnp.int32, (block, confs), 0) + b * block == key)
            .astype(F32)
            .astype(BF16)
        )
        picked = jnp.dot(onehot, dets, preferred_element_type=F32)
        for h in range(2):
            inter_ref[pl.ds(h, block, stride=2), :] = picked[:, h * 128 : (h + 1) * 128]
        out_ref[pl.ds(b * 2 * block, 2 * block), :] = inter_ref[...].astype(BF16)


def pack(coef, labels, transforms, capacity):
    confs = coef.shape[1]
    rows = 2 * 3 * confs
    return pl.pallas_call(
        functools.partial(pack_kernel, capacity),
        out_shape=(
            jax.ShapeDtypeStruct((rows, 128), BF16),
            jax.ShapeDtypeStruct((1, confs), jnp.int32),
        ),
        scratch_shapes=[pltpu.VMEM((512, 128), F32)],
        compiler_params=pltpu.CompilerParams(vmem_limit_bytes=VMEM_LIMIT),
        name="pack",
    )(coef, labels, transforms)


def build_table(slab_refs, table_ref, stage_ref):
    blocks, rows, _ = slab_refs[0].shape
    lanes = rows // 3

    def build(j, carry):
        for h, slab_ref in enumerate(slab_refs):
            stage_ref[...] = slab_ref[j].astype(F32)
            for ct in range(3):
                piece = stage_ref[pl.ds(ct, lanes, stride=3), :]
                piece = jnp.concatenate([piece, jnp.zeros((128 - lanes, 128), F32)], axis=0)
                start = (j * 3 + ct) * 256 + (PAD + h)
                table_ref[pl.ds(start, 128, stride=2), :] = piece.T
        return carry

    lax.fori_loop(0, blocks, build, 0)


def plan_kernel(steps, width, tgt_ref, val_ref, cnt_ref, out_ref):
    exc, length = tgt_ref.shape
    counts = cnt_ref[...]
    place = lax.broadcasted_iota(jnp.int32, (1, length), 1)
    key = counts * 4096 + (4095 - place)
    key8 = jnp.broadcast_to(key, (8, length)).astype(F32)
    slots = lax.broadcasted_iota(jnp.int32, (exc, length), 0)
    live = jnp.where(slots < counts, val_ref[...].astype(F32), 0.0)
    tgt = tgt_ref[...]
    high = tgt >> 7
    rows = lax.broadcasted_iota(jnp.int32, (8, length), 0)
    extra = jnp.where(rows == 0, place >> 7, jnp.where(rows == 1, place & 127, 0))
    lists = jnp.concatenate(
        [high.astype(F32), (tgt & 127).astype(F32), live, extra.astype(F32)], axis=0
    ).astype(BF16)
    total = jnp.zeros((lists.shape[0], length), F32)
    for k in range(length // 128):
        mine = key8[:, k * 128 : (k + 1) * 128]
        column = jnp.concatenate([mine] * 16, axis=0).T[:, 0:1]
        ahead = jnp.where(key8[0:1, :] > column, 1.0, 0.0)
        rank = jnp.sum(ahead, axis=1, keepdims=True).astype(jnp.int32)
        moved = (
            (lax.broadcasted_iota(jnp.int32, (128, length), 1) == rank).astype(F32).astype(BF16)
        )
        total = total + jnp.dot(
            lists[:, k * 128 : (k + 1) * 128], moved, preferred_element_type=F32
        )
    lane = lax.broadcasted_iota(jnp.int32, (8, length), 1)
    bounds = jnp.zeros((8, length), F32)
    for k in range(exc // steps):
        over = jnp.sum(jnp.where(counts > k * steps, 1.0, 0.0), axis=1, keepdims=True)
        groups = ((over.astype(jnp.int32) + (width - 1)) // width).astype(F32)
        bounds = jnp.where(jnp.logical_and(lane == k, rows == 2), groups, bounds)
    out_ref[0 : 3 * exc, :] = total[: 3 * exc]
    out_ref[3 * exc :, :] = jnp.where(rows == 2, bounds, total[3 * exc :])


def plan(targets, values, counts, steps, width):
    exc, length = targets.shape
    return pl.pallas_call(
        functools.partial(plan_kernel, steps, width),
        out_shape=jax.ShapeDtypeStruct((3 * exc + 8, length), F32),
        compiler_params=pltpu.CompilerParams(vmem_limit_bytes=VMEM_LIMIT),
        name="plan",
    )(targets, values, counts[None, :])


def beta_block(table_ref, tgt_ref, row_ref, w_ref, out_refs, wt_ref, acc_ref):
    lanes = out_refs[0].shape[1] // 3
    exc = 16
    cols = 384
    slot = lax.broadcasted_iota(jnp.int32, (8, 128), 0) >> 1
    for ct in range(3):
        turned = jnp.concatenate(
            [w_ref[0, pl.ds(ct, exc, stride=3), :], jnp.zeros((128 - exc, 128), F32)], axis=0
        ).T
        for h in range(2):
            wt_ref[pl.ds(ct * 256 + h, 128, stride=2), :] = turned
    buckets = exc // STEPS
    at = (exc + 1) * cols

    def make(depth):
        def group(g, carry):
            near = tgt_ref.at[pl.ds(g * FEW, exc * cols)]
            for v in range(FEW // 4):
                first = pl.multiple_of(g * (2 * FEW) + v * 8, 8)
                w8 = wt_ref[pl.ds(first, 8), :]
                acc = jnp.zeros((8, 128), F32)
                for e in range(depth):
                    got = None
                    for s in range(4):
                        t = near[e * cols + 4 * v + s]
                        win = table_ref[pl.ds(t + (PAD - 2 * s), 8), :]
                        got = win if s == 0 else jnp.where(slot == s, win, got)
                    acc = acc + got * w8[:, e : e + 1]
                acc_ref[pl.ds(first, 8), :] = acc
            return carry

        return group

    for k in reversed(range(buckets)):
        begin = tgt_ref[at + k + 1] >> 1 if k + 1 < buckets else 0
        lax.fori_loop(begin, tgt_ref[at + k] >> 1, make((k + 1) * STEPS), 0)
    ids = jnp.concatenate([row_ref[0, exc * 3 + ct : exc * 3 + ct + 1, :] for ct in range(3)], axis=1)
    back = (
        (lax.broadcasted_iota(jnp.int32, (cols, cols), 0) * 2 == ids).astype(F32).astype(BF16)
    )
    for h, out_ref in enumerate(out_refs):
        left = acc_ref[pl.ds(h, cols, stride=2), :].T
        done = jnp.zeros((128, cols), F32)
        for _ in range(3):
            piece = left.astype(BF16)
            done = done + lax.dot_general(
                piece, back, (((1,), (1,)), ((), ())), preferred_element_type=F32
            )
            left = left - piece.astype(F32)
        for ct in range(3):
            out_ref[0, pl.ds(ct, lanes, stride=3), :] = done[:lanes, ct * 128 : (ct + 1) * 128]


def beta_first_kernel(
    x_ref, y_ref, tgt_ref, row_ref, w_ref, own_ref, far_ref, table_ref, wt_ref, acc_ref, stage_ref
):
    @pl.when(pl.program_id(0) == 0)
    def _():
        build_table((x_ref, y_ref), table_ref, stage_ref)

    beta_block(table_ref, tgt_ref, row_ref, w_ref, (own_ref, far_ref), wt_ref, acc_ref)


def beta_rest_kernel(
    table_ref, tgt_ref, row_ref, w_ref, old_own, old_far, own_ref, far_ref, wt_ref, acc_ref
):
    beta_block(table_ref, tgt_ref, row_ref, w_ref, (own_ref, far_ref), wt_ref, acc_ref)


def list_specs(skip):
    return [
        pl.BlockSpec((8192,), lambda j: (j + skip,), memory_space=pltpu.SMEM),
        pl.BlockSpec((1, 64, 128), lambda j: (j + skip, 0, 0)),
        pl.BlockSpec((1, 48, 128), lambda j: (j + skip, 0, 0)),
    ]


def beta_params(blocks):
    return dict(
        compiler_params=pltpu.CompilerParams(vmem_limit_bytes=VMEM_LIMIT),
        cost_estimate=pl.CostEstimate(
            flops=blocks * 8 * 10**8, bytes_accessed=blocks * 2**20, transcendentals=0
        ),
    )


def beta_first(x2, y2, numbers, weights, blocks):
    nbeta, rows, _ = x2.shape
    half = numbers.shape[0]
    height = 2 * nbeta * 384 + 2 * PAD
    piece = pl.BlockSpec((1, rows, 128), lambda j: (j, 0, 0))
    slab = pl.BlockSpec((nbeta, rows, 128), lambda j: (0, 0, 0))
    return pl.pallas_call(
        beta_first_kernel,
        out_shape=(
            jax.ShapeDtypeStruct((half, rows, 128), F32),
            jax.ShapeDtypeStruct((half, rows, 128), F32),
            jax.ShapeDtypeStruct((height, 128), F32),
        ),
        grid=(blocks,),
        in_specs=[slab, slab] + list_specs(0),
        out_specs=(piece, piece, pl.BlockSpec((height, 128), lambda j: (0, 0))),
        scratch_shapes=[
            pltpu.VMEM((768, 128), F32),
            pltpu.VMEM((768, 128), F32),
            pltpu.VMEM((rows, 128), F32),
        ],
        name="beta_first",
        **beta_params(blocks),
    )(x2, y2, numbers.reshape(-1), numbers, weights)


def beta_rest(table, numbers, weights, own, far, skip):
    half, rows, _ = own.shape
    piece = pl.BlockSpec((1, rows, 128), lambda j: (j + skip, 0, 0))
    return pl.pallas_call(
        beta_rest_kernel,
        out_shape=(
            jax.ShapeDtypeStruct(own.shape, F32),
            jax.ShapeDtypeStruct(own.shape, F32),
        ),
        grid=(half - skip,),
        in_specs=[pl.BlockSpec(table.shape, lambda j: (0, 0))]
        + list_specs(skip)
        + [pl.BlockSpec(memory_space=pl.ANY)] * 2,
        out_specs=(piece, piece),
        scratch_shapes=[pltpu.VMEM((768, 128), F32), pltpu.VMEM((768, 128), F32)],
        input_output_aliases={4: 0, 5: 1},
        name="beta_rest",
        **beta_params(half - skip),
    )(table, numbers.reshape(-1), numbers, weights, own, far)


def alpha_kernel(
    own_ref,
    tbl_hbm,
    tgt_ref,
    w_ref,
    diag_ref,
    order_ref,
    out_ref,
    table_ref,
    wt_ref,
    acc_ref,
    buf_ref,
    sem,
):
    chunk = buf_ref.shape[1]
    total = tbl_hbm.shape[0]
    n = total // chunk
    exc = w_ref.shape[0]
    rows = diag_ref.shape[0]

    def fetch(k):
        return pltpu.make_async_copy(
            tbl_hbm.at[pl.ds(k * chunk, chunk), :], buf_ref.at[k], sem.at[k]
        )

    for k in range(n):
        fetch(k).start()
    for k in range(rows // 128):
        turned = jnp.concatenate(
            [w_ref[:, k * 128 : (k + 1) * 128], jnp.zeros((128 - exc, 128), F32)], axis=0
        ).T
        for ct in range(3):
            wt_ref[pl.ds(k * 384 + ct, 128, stride=3), :] = turned

    for k in range(n):
        fetch(k).wait()

        def widen(i, carry):
            start = pl.multiple_of(i * 128, 128)
            table_ref[pl.ds(pl.multiple_of(start + (k * chunk + PAD), 8), 128), :] = buf_ref[
                k, pl.ds(start, 128), :
            ].astype(F32)
            return carry

        lax.fori_loop(0, chunk // 128, widen, 0)
    sub = lax.broadcasted_iota(jnp.int32, (8, 128), 0)
    buckets = exc // STEPS
    ids = exc * rows
    at = ids + rows

    front = sub < 3
    back = jnp.logical_and(sub >= 3, sub < 6)

    def make(depth):
        def group(g, carry):
            first = pl.multiple_of(g * WIDE, WIDE)
            near = tgt_ref.at[pl.ds(first, ids + WIDE)]
            w6 = [wt_ref[pl.ds(first * 3 + 6 * q, 8), :] for q in range(WIDE // 2)]
            acc = [jnp.zeros((8, 128), F32)] * (WIDE // 2)
            for e in range(depth):
                for q in range(WIDE // 2):
                    low = table_ref[pl.ds(near[e * rows + 2 * q] + PAD, 8), :]
                    high = table_ref[pl.ds(near[e * rows + 2 * q + 1] + (PAD - 3), 8), :]
                    w = jnp.broadcast_to(w6[q][:, e : e + 1], (8, 128))
                    acc[q] = acc[q] + jnp.where(front, low, high) * w
            for q in range(WIDE // 2):
                low = near[ids + 2 * q] + PAD
                high = near[ids + 2 * q + 1] + (PAD - 3)
                pltpu.store(acc_ref.at[pl.ds(low, 8), :], acc[q], mask=front)
                pltpu.store(acc_ref.at[pl.ds(high, 8), :], acc[q], mask=back)
            return carry

        return group

    for k in reversed(range(buckets)):
        begin = tgt_ref[at + k + 1] if k + 1 < buckets else 0
        lax.fori_loop(begin, tgt_ref[at + k], make((k + 1) * STEPS), 0)

    own = own_ref[0]

    def finish(i, carry):
        for u in range(4):
            place = pl.multiple_of(i * 32 + u * 8, 8)
            for ct in range(3):
                spot = place * 3 + (ct + PAD)
                out_ref[pl.ds(place * 3 + ct, 8, stride=3), :] = (
                    acc_ref[pl.ds(spot, 8, stride=3), :]
                    + diag_ref[pl.ds(place, 8), ct * 128 : (ct + 1) * 128]
                    * table_ref[pl.ds(own * 3 + spot, 8, stride=3), :]
                )
        return carry

    lax.fori_loop(0, rows // 32, finish, 0)


def alpha_term(own, table, numbers, weights, diag, order):
    rows = diag.shape[0]
    total = table.shape[0]
    chunk = total // 8
    return pl.pallas_call(
        alpha_kernel,
        out_shape=jax.ShapeDtypeStruct((rows * 3, 128), F32),
        in_specs=[
            pl.BlockSpec(memory_space=pltpu.SMEM),
            pl.BlockSpec(memory_space=pl.ANY),
            pl.BlockSpec(memory_space=pltpu.SMEM),
            pl.BlockSpec(memory_space=pltpu.VMEM),
            pl.BlockSpec(memory_space=pltpu.VMEM),
            pl.BlockSpec(memory_space=pl.ANY),
        ],
        out_specs=pl.BlockSpec(memory_space=pltpu.VMEM),
        scratch_shapes=[
            pltpu.VMEM((total + 4 * PAD, 128), F32),
            pltpu.VMEM((rows * 3 + PAD, 128), F32),
            pltpu.VMEM((rows * 3 + 4 * PAD, 128), F32),
            pltpu.VMEM((8, chunk, 128), BF16),
            pltpu.SemaphoreType.DMA((8,)),
        ],
        compiler_params=pltpu.CompilerParams(vmem_limit_bytes=VMEM_LIMIT),
        cost_estimate=pl.CostEstimate(
            flops=10**10, bytes_accessed=16 * 2**20, transcendentals=0
        ),
        name="alpha_term",
    )(own, table, numbers, weights, diag, order)


def merge_kernel(nalpha, alpha_ref, beta_ref, out_ref):
    nbeta = beta_ref.shape[0]
    pieces = out_ref.shape[1]

    def senders(beta_s, carry):
        for alpha_s in range(nalpha):
            p = alpha_s * nbeta + beta_s
            one = alpha_ref[pl.ds(p * pieces, pieces), :]
            other = beta_ref[beta_s, alpha_s * pieces : (alpha_s + 1) * pieces, :]
            out_ref[p] = (one + other).astype(BF16)
        return carry

    lax.fori_loop(0, nbeta, senders, 0)


def merge(alpha, beta, nalpha, pieces):
    devices = nalpha * beta.shape[0]
    return pl.pallas_call(
        functools.partial(merge_kernel, nalpha),
        out_shape=jax.ShapeDtypeStruct((devices, pieces, 128), BF16),
        compiler_params=pltpu.CompilerParams(vmem_limit_bytes=VMEM_LIMIT),
        name="merge",
    )(alpha, beta)


def finish_kernel(entries, parts_ref, sigma_ref, coef_ref, out_ref, rms_ref):
    parts = parts_ref[:, 0, :]
    square = parts[:, 0:1]
    total = jnp.sum(parts, axis=0, keepdims=True)
    rayleigh = total[:, 1:2] / total[:, 0:1]
    shift = rayleigh - parts[:, 3:4]
    rest = jnp.sum(parts[:, 2:3] + shift * shift * square, axis=0, keepdims=True)
    out_ref[...] = sigma_ref[...] - rayleigh * coef_ref[...]
    rms_ref[...] = jnp.sqrt(rest / entries)


def finish(parts, sigma, coef, entries):
    return pl.pallas_call(
        functools.partial(finish_kernel, float(entries)),
        out_shape=(
            jax.ShapeDtypeStruct(sigma.shape, F32),
            jax.ShapeDtypeStruct((1, 1), F32),
        ),
        name="finish",
    )(parts, sigma, coef)


def unpack_kernel(
    r_ref, key_ref, label_ref, coef_ref, tr_ref, sigma_ref, part_ref, stage_ref, half_ref
):
    devices, pieces, _ = r_ref.shape
    rows = devices * pieces // 2
    confs = key_ref.shape[1]
    width = coef_ref.shape[0]
    ncls = tr_ref.shape[0]
    tall = width + -width % 8

    def spread(p, carry):
        stage_ref[pl.ds(p * pieces, pieces), :] = r_ref[p].astype(F32)
        return carry

    lax.fori_loop(0, devices, spread, 0)
    for h in range(2):
        half_ref[:, h * 128 : (h + 1) * 128] = stage_ref[pl.ds(h, rows, stride=2), :].astype(BF16)
    key = key_ref[...]
    block = 256
    dets = jnp.zeros((256, confs), F32)
    for b in range(rows // block):
        onehot = (
            (lax.broadcasted_iota(jnp.int32, (block, confs), 0) + b * block == key)
            .astype(F32)
            .astype(BF16)
        )
        dets = dets + lax.dot_general(
            half_ref[pl.ds(b * block, block), :],
            onehot,
            (((0,), (0,)), ((), ())),
            preferred_element_type=F32,
        )
    trans = jnp.concatenate([padded(tr_ref, c) for c in range(ncls)], axis=0)
    products = jnp.dot(trans, dets, precision=HIGH, preferred_element_type=F32)
    sigma = jnp.zeros((width, confs), F32)
    for c in range(ncls):
        part = products[c * tall : c * tall + width]
        sigma = sigma + jnp.where(label_ref[0:1, :] == c, part, 0.0)
    coef = coef_ref[...]
    sigma_ref[...] = sigma
    square = jnp.sum(jnp.sum(coef * coef, axis=1, keepdims=True), axis=0, keepdims=True)
    cross = jnp.sum(jnp.sum(coef * sigma, axis=1, keepdims=True), axis=0, keepdims=True)
    ratio = jnp.where(square > 0.0, cross / jnp.where(square > 0.0, square, 1.0), 0.0)
    rest = sigma - ratio * coef
    rho = jnp.sum(jnp.sum(rest * rest, axis=1, keepdims=True), axis=0, keepdims=True)
    lane = lax.broadcasted_iota(jnp.int32, (1, 128), 1)
    part_ref[...] = jnp.where(
        lane == 0,
        square,
        jnp.where(lane == 1, cross, jnp.where(lane == 2, rho, jnp.where(lane == 3, ratio, 0.0))),
    )


def unpack(returned, key, labels, coef, transforms):
    return pl.pallas_call(
        unpack_kernel,
        out_shape=(
            jax.ShapeDtypeStruct(coef.shape, F32),
            jax.ShapeDtypeStruct((1, 128), F32),
        ),
        scratch_shapes=[
            pltpu.VMEM((returned.shape[0] * returned.shape[1], 128), F32),
            pltpu.VMEM((returned.shape[0] * returned.shape[1] // 2, 256), BF16),
        ],
        compiler_params=pltpu.CompilerParams(vmem_limit_bytes=VMEM_LIMIT),
        name="unpack",
    )(returned, key, labels, coef, transforms)


def exchange(x, axes):
    return lax.all_to_all(x, axes, split_axis=0, concat_axis=0, tiled=True)


def body(
    csf_coef,
    conf_class,
    conf_tile,
    transforms,
    alpha_targets,
    alpha_values,
    alpha_counts,
    beta_targets,
    beta_values,
    beta_counts,
    det_diag,
):
    nalpha = lax.axis_size("alpha")
    nbeta = lax.axis_size("beta")
    devices = nalpha * nbeta
    ncsf, confs = csf_coef.shape
    capacity = 3 * confs // devices
    rows_alpha = det_diag.shape[0]
    width = transforms.shape[2]
    exc = alpha_targets.shape[0]
    pieces = capacity * width // 128
    labels = jnp.stack([conf_class, conf_tile[:, 0]])
    bplan = plan(beta_targets, beta_values, beta_counts, STEPS, FEW)
    zero = jnp.zeros((1, bplan.shape[1]), F32)
    lists = jnp.concatenate(
        [
            bplan[:exc],
            bplan[3 * exc : 3 * exc + 1],
            zero,
            bplan[exc : 2 * exc],
            bplan[3 * exc + 1 : 3 * exc + 3],
            bplan[2 * exc : 3 * exc],
        ],
        axis=0,
    ).astype(BF16)
    lists = lists.reshape(-1, 128)
    lists = jnp.pad(lists, ((0, -lists.shape[0] % 16), (0, 0)))
    aplan = plan(alpha_targets, alpha_values, alpha_counts, STEPS, WIDE)
    anumbers = jnp.concatenate(
        [
            aplan[:exc] * 384.0 + aplan[exc : 2 * exc] * 3.0,
            aplan[3 * exc : 3 * exc + 1] * 384.0 + aplan[3 * exc + 1 : 3 * exc + 2] * 3.0,
            aplan[3 * exc + 2 : 3 * exc + 3],
        ],
        axis=0,
    )
    anumbers = anumbers.astype(jnp.int32).reshape(-1)
    aweights = aplan[2 * exc : 3 * exc]

    body_rows = nalpha * pieces
    heard = exchange(jnp.broadcast_to(lists[None], (nbeta,) + lists.shape), "beta")
    labels, lists = lax.optimization_barrier((labels, lists))
    outgoing, key = pack(csf_coef, labels, transforms, capacity)
    outgoing, heard = lax.optimization_barrier((outgoing, heard))
    slab = exchange(outgoing.reshape(nalpha, nbeta * pieces, 128), "alpha")
    slab, anumbers, aweights = lax.optimization_barrier((slab, anumbers, aweights))
    x2 = (
        slab.reshape(nalpha, nbeta, pieces, 128)
        .transpose(1, 0, 2, 3)
        .reshape(nbeta, body_rows, 128)
    )
    nrows = (exc + 2) * (bplan.shape[1] // 128)
    wrows = exc * (bplan.shape[1] // 128)
    half = nbeta // 2
    side = lax.axis_index("alpha") % 2
    swap = [(i, i ^ 1) for i in range(nalpha)]
    y2 = lax.ppermute(x2, "alpha", swap)
    mine = lax.dynamic_slice_in_dim(heard, side * half, half, axis=0)
    high = mine[:, :nrows].astype(jnp.int32)
    low = mine[:, nrows : 2 * nrows].astype(jnp.int32)
    bnumbers = jnp.pad(high * 256 + low * 2, ((0, 0), (0, 64 - nrows), (0, 0)))
    bweights = mine[:, 2 * nrows : 2 * nrows + wrows].astype(F32)

    got = exchange(x2, "beta")
    near_a, far_a, btable = beta_first(x2, y2, bnumbers, bweights, FIRST)
    got, btable = lax.optimization_barrier((got, btable))
    flat = (
        got.reshape(nbeta, nalpha, pieces, 128).transpose(1, 0, 2, 3).reshape(-1, 128)
    )
    table = lax.all_gather(flat, "alpha", axis=0, tiled=True)
    near_b, far_b = beta_rest(btable, bnumbers, bweights, near_a, far_a, FIRST)
    back = lax.ppermute(far_b, "alpha", swap)
    beta_slab = jnp.where(
        side == 0,
        jnp.concatenate([near_b, back], axis=0),
        jnp.concatenate([back, near_b], axis=0),
    )
    beta_tile = exchange(beta_slab, "beta")
    own = (lax.axis_index("alpha") * rows_alpha).astype(jnp.int32)[None]
    partial = alpha_term(own, table, anumbers, aweights, det_diag, beta_slab)
    sigma_tile = merge(partial, beta_tile, nalpha, pieces)
    returned = exchange(sigma_tile, BOTH)
    sigma, part = unpack(returned, key, labels, csf_coef, transforms)
    parts = exchange(jnp.broadcast_to(part[None], (devices, 1, 128)), BOTH)
    residual, rms = finish(parts, sigma, csf_coef, ncsf * confs * devices)
    return (residual, rms[0, 0])


def solution(mesh):
    placed = (
        P(None, BOTH),
        P(BOTH),
        P(BOTH, None),
        P(),
        P(None, "alpha"),
        P(None, "alpha"),
        P("alpha"),
        P(None, "beta"),
        P(None, "beta"),
        P("beta"),
        P("alpha", "beta"),
    )
    return jax.shard_map(
        body,
        mesh=mesh,
        in_specs=placed,
        out_specs=(P(None, BOTH), P()),
        check_vma=False,
    )
```

```python
import functools

import jax
import jax.numpy as jnp
from jax import lax
from jax.experimental import pallas as pl
from jax.experimental.pallas import tpu as pltpu
from jax.sharding import PartitionSpec as P


F32 = jnp.float32
BF16 = jnp.bfloat16
HIGH = lax.Precision.HIGHEST
BOTH = ("alpha", "beta")
PAD = 8
FIRST = 1
STEPS = 2
WIDE = 32
FEW = 16
VMEM_LIMIT = 60 * 1024 * 1024


def stacked(coef, classes, classes_n):
    parts = []
    for c in range(classes_n):
        parts.append(jnp.where(classes == c, coef, jnp.zeros_like(coef)))
    return jnp.concatenate(parts, axis=0)


def padded(ref, index=None):
    value = ref[...] if index is None else ref[index]
    fill = -value.shape[0] % 8
    return jnp.concatenate([value, jnp.zeros((fill, value.shape[1]), F32)], axis=0)


def pack_kernel(capacity, coef_ref, label_ref, tr_ref, out_ref, key_ref, inter_ref):
    confs = coef_ref.shape[1]
    ncls = tr_ref.shape[0]
    devices = confs * 3 // capacity
    masked = stacked(padded(coef_ref), label_ref[0:1, :], ncls)
    trans = jnp.concatenate([padded(tr_ref, c) for c in range(ncls)], axis=0)
    dets = lax.dot_general(
        masked, trans, (((0,), (0,)), ((), ())), precision=HIGH, preferred_element_type=F32
    ).astype(BF16)
    tile = label_ref[1:2, :]
    hit = lax.broadcasted_iota(jnp.int32, (devices, confs), 0) == tile
    before = lax.broadcasted_iota(jnp.int32, (confs, confs), 0) < lax.broadcasted_iota(
        jnp.int32, (confs, confs), 1
    )
    counts = jnp.dot(
        hit.astype(F32).astype(BF16), before.astype(F32).astype(BF16), preferred_element_type=F32
    )
    slot = jnp.sum(jnp.where(hit, counts, 0.0), axis=0, keepdims=True).astype(jnp.int32)
    key = tile * capacity + slot
    key_ref[...] = key
    rows = devices * capacity
    block = 256
    for b in range(rows // block):
        onehot = (
            (lax.broadcasted_iota(jnp.int32, (block, confs), 0) + b * block == key)
            .astype(F32)
            .astype(BF16)
        )
        picked = jnp.dot(onehot, dets, preferred_element_type=F32)
        for h in range(2):
            inter_ref[pl.ds(h, block, stride=2), :] = picked[:, h * 128 : (h + 1) * 128]
        out_ref[pl.ds(b * 2 * block, 2 * block), :] = inter_ref[...].astype(BF16)


def pack(coef, labels, transforms, capacity):
    confs = coef.shape[1]
    rows = 2 * 3 * confs
    return pl.pallas_call(
        functools.partial(pack_kernel, capacity),
        out_shape=(
            jax.ShapeDtypeStruct((rows, 128), BF16),
            jax.ShapeDtypeStruct((1, confs), jnp.int32),
        ),
        scratch_shapes=[pltpu.VMEM((512, 128), F32)],
        compiler_params=pltpu.CompilerParams(vmem_limit_bytes=VMEM_LIMIT),
        name="pack",
    )(coef, labels, transforms)


def build_table(slab_refs, table_ref, stage_ref):
    blocks, rows, _ = slab_refs[0].shape
    lanes = rows // 3

    def build(j, carry):
        for h, slab_ref in enumerate(slab_refs):
            stage_ref[...] = slab_ref[j].astype(F32)
            for ct in range(3):
                piece = stage_ref[pl.ds(ct, lanes, stride=3), :]
                piece = jnp.concatenate([piece, jnp.zeros((128 - lanes, 128), F32)], axis=0)
                start = (j * 3 + ct) * 256 + (PAD + h)
                table_ref[pl.ds(start, 128, stride=2), :] = piece.T
        return carry

    lax.fori_loop(0, blocks, build, 0)


def plan_kernel(steps, width, tgt_ref, val_ref, cnt_ref, out_ref, *row_refs):
    exc, length = tgt_ref.shape
    counts = cnt_ref[...]
    place = lax.broadcasted_iota(jnp.int32, (1, length), 1)
    key = counts * 4096 + (4095 - place)
    key8 = jnp.broadcast_to(key, (8, length)).astype(F32)
    slots = lax.broadcasted_iota(jnp.int32, (exc, length), 0)
    live = jnp.where(slots < counts, val_ref[...].astype(F32), 0.0)
    tgt = tgt_ref[...]
    high = tgt >> 7
    rows = lax.broadcasted_iota(jnp.int32, (8, length), 0)
    extra = jnp.where(rows == 0, place >> 7, jnp.where(rows == 1, place & 127, 0))
    lists = jnp.concatenate(
        [high.astype(F32), (tgt & 127).astype(F32), live, extra.astype(F32)], axis=0
    ).astype(BF16)
    total = jnp.zeros((lists.shape[0], length), F32)
    for k in range(length // 128):
        mine = key8[:, k * 128 : (k + 1) * 128]
        column = jnp.concatenate([mine] * 16, axis=0).T[:, 0:1]
        ahead = jnp.where(key8[0:1, :] > column, 1.0, 0.0)
        rank = jnp.sum(ahead, axis=1, keepdims=True).astype(jnp.int32)
        moved = (
            (lax.broadcasted_iota(jnp.int32, (128, length), 1) == rank).astype(F32).astype(BF16)
        )
        total = total + jnp.dot(
            lists[:, k * 128 : (k + 1) * 128], moved, preferred_element_type=F32
        )
    lane = lax.broadcasted_iota(jnp.int32, (8, length), 1)
    bounds = jnp.zeros((8, length), F32)
    for k in range(exc // steps):
        over = jnp.sum(jnp.where(counts > k * steps, 1.0, 0.0), axis=1, keepdims=True)
        groups = ((over.astype(jnp.int32) + (width - 1)) // width).astype(F32)
        bounds = jnp.where(jnp.logical_and(lane == k, rows == 2), groups, bounds)
    tail = jnp.where(rows == 2, bounds, total[3 * exc :])
    if not row_refs:
        out_ref[0 : 3 * exc, :] = total[: 3 * exc]
        out_ref[3 * exc :, :] = tail
        return
    (row_ref,) = row_refs
    row_ref[...] = jnp.zeros_like(row_ref)
    parts = length // 128
    for ct in range(parts):
        lanes = slice(ct * 128, (ct + 1) * 128)
        for k in range(3):
            row_ref[pl.ds(k * 64 + ct, exc, stride=parts), :] = total[
                k * exc : (k + 1) * exc, lanes
            ]
        high_row = exc * parts + ct
        row_ref[high_row : high_row + 1, :] = tail[0:1, lanes]
        row_ref[64 + high_row : 65 + high_row, :] = tail[1:2, lanes]
        bound_row = 64 + (exc + 1) * parts + ct
        row_ref[bound_row : bound_row + 1, :] = tail[2:3, lanes]
    out_ref[...] = row_ref[...].astype(BF16)


def plan(targets, values, counts, steps, width, packed):
    exc, length = targets.shape
    wanted = jax.ShapeDtypeStruct((3 * exc + 8, length), F32)
    return pl.pallas_call(
        functools.partial(plan_kernel, steps, width),
        out_shape=jax.ShapeDtypeStruct((256, 128), BF16) if packed else wanted,
        scratch_shapes=[pltpu.VMEM((256, 128), F32)] if packed else [],
        compiler_params=pltpu.CompilerParams(vmem_limit_bytes=VMEM_LIMIT),
        name="plan",
    )(targets, values, counts[None, :])


def beta_block(table_ref, tgt_ref, row_ref, w_ref, out_refs, wt_ref, acc_ref, wide_ref):
    lanes = out_refs[0].shape[1] // 3
    exc = 16
    cols = 384
    slot = lax.broadcasted_iota(jnp.int32, (8, 128), 0) >> 1
    wide_ref[...] = w_ref[0].astype(F32)
    for ct in range(3):
        turned = jnp.concatenate(
            [wide_ref[pl.ds(ct, exc, stride=3), :], jnp.zeros((128 - exc, 128), F32)], axis=0
        ).T
        for h in range(2):
            wt_ref[pl.ds(ct * 256 + h, 128, stride=2), :] = turned
    buckets = exc // STEPS
    at = (exc + 1) * cols

    def make(depth):
        def group(g, carry):
            near = tgt_ref.at[pl.ds(g * FEW, exc * cols)]
            for v in range(FEW // 4):
                first = pl.multiple_of(g * (2 * FEW) + v * 8, 8)
                w8 = wt_ref[pl.ds(first, 8), :]
                acc = jnp.zeros((8, 128), F32)
                for e in range(depth):
                    got = None
                    for s in range(4):
                        t = near[e * cols + 4 * v + s]
                        win = table_ref[pl.ds(t + (PAD - 2 * s), 8), :]
                        got = win if s == 0 else jnp.where(slot == s, win, got)
                    acc = acc + got * w8[:, e : e + 1]
                acc_ref[pl.ds(first, 8), :] = acc
            return carry

        return group

    for k in reversed(range(buckets)):
        begin = tgt_ref[at + k + 1] >> 1 if k + 1 < buckets else 0
        lax.fori_loop(begin, tgt_ref[at + k] >> 1, make((k + 1) * STEPS), 0)
    ids = jnp.concatenate([row_ref[0, exc * 3 + ct : exc * 3 + ct + 1, :] for ct in range(3)], axis=1)
    back = (
        (lax.broadcasted_iota(jnp.int32, (cols, cols), 0) * 2 == ids).astype(F32).astype(BF16)
    )
    for h, out_ref in enumerate(out_refs):
        left = acc_ref[pl.ds(h, cols, stride=2), :].T
        done = jnp.zeros((128, cols), F32)
        for _ in range(3):
            piece = left.astype(BF16)
            done = done + lax.dot_general(
                piece, back, (((1,), (1,)), ((), ())), preferred_element_type=F32
            )
            left = left - piece.astype(F32)
        for ct in range(3):
            out_ref[0, pl.ds(ct, lanes, stride=3), :] = done[:lanes, ct * 128 : (ct + 1) * 128]


def table_kernel(x_ref, y_ref, table_ref, stage_ref):
    build_table((x_ref, y_ref), table_ref, stage_ref)


def slab_table(x2, y2):
    nbeta, rows, _ = x2.shape
    return pl.pallas_call(
        table_kernel,
        out_shape=jax.ShapeDtypeStruct((2 * nbeta * 384 + 2 * PAD, 128), F32),
        in_specs=[pl.BlockSpec(memory_space=pltpu.VMEM)] * 2,
        out_specs=pl.BlockSpec(memory_space=pltpu.VMEM),
        scratch_shapes=[pltpu.VMEM((rows, 128), F32)],
        compiler_params=pltpu.CompilerParams(vmem_limit_bytes=VMEM_LIMIT),
        cost_estimate=pl.CostEstimate(flops=10**9, bytes_accessed=2**23, transcendentals=0),
        name="slab_table",
    )(x2, y2)


def beta_kernel(side_ref, table_ref, tgt_ref, row_ref, w_ref, *refs):
    own_ref, far_ref, wt_ref, acc_ref, wide_ref = refs[-5:]
    beta_block(
        table_ref, tgt_ref, row_ref, w_ref, (own_ref, far_ref), wt_ref, acc_ref, wide_ref
    )


def beta_term(side, table, numbers, heard, rows, skip, blocks, old):
    half = numbers.shape[0]
    nbeta = heard.shape[0]
    near = pl.BlockSpec((1, rows, 128), lambda j, side: (side[0] * half + j + skip, 0, 0))
    far = pl.BlockSpec((1, rows, 128), lambda j, side: (j + skip, 0, 0))
    return pl.pallas_call(
        beta_kernel,
        out_shape=(
            jax.ShapeDtypeStruct((nbeta, rows, 128), F32),
            jax.ShapeDtypeStruct((half, rows, 128), F32),
        ),
        grid_spec=pltpu.PrefetchScalarGridSpec(
            num_scalar_prefetch=1,
            grid=(blocks,),
            in_specs=[
                pl.BlockSpec(table.shape, lambda j, side: (0, 0)),
                pl.BlockSpec((8192,), lambda j, side: (j + skip,), memory_space=pltpu.SMEM),
                pl.BlockSpec((1, 64, 128), lambda j, side: (j + skip, 0, 0)),
                pl.BlockSpec((1, 64, 128), lambda j, side: (side[0] * half + j + skip, 2, 0)),
            ]
            + [pl.BlockSpec(memory_space=pl.ANY)] * len(old),
            out_specs=(near, far),
            scratch_shapes=[
                pltpu.VMEM((768, 128), F32),
                pltpu.VMEM((768, 128), F32),
                pltpu.VMEM((64, 128), F32),
            ],
        ),
        input_output_aliases={5: 0, 6: 1} if old else {},
        compiler_params=pltpu.CompilerParams(vmem_limit_bytes=VMEM_LIMIT),
        cost_estimate=pl.CostEstimate(
            flops=blocks * 8 * 10**8, bytes_accessed=blocks * 2**20, transcendentals=0
        ),
        name="beta_rest" if old else "beta_first",
    )(side, table, numbers.reshape(-1), numbers, heard, *old)


def alpha_kernel(
    own_ref,
    tbl_hbm,
    tgt_ref,
    w_ref,
    diag_ref,
    order_ref,
    out_ref,
    table_ref,
    wt_ref,
    acc_ref,
    buf_ref,
    sem,
):
    chunk = buf_ref.shape[1]
    total = tbl_hbm.shape[0]
    n = total // chunk
    exc = w_ref.shape[0]
    rows = diag_ref.shape[0]

    def fetch(k):
        return pltpu.make_async_copy(
            tbl_hbm.at[pl.ds(k * chunk, chunk), :], buf_ref.at[k], sem.at[k]
        )

    for k in range(n):
        fetch(k).start()
    for k in range(rows // 128):
        turned = jnp.concatenate(
            [w_ref[:, k * 128 : (k + 1) * 128], jnp.zeros((128 - exc, 128), F32)], axis=0
        ).T
        for ct in range(3):
            wt_ref[pl.ds(k * 384 + ct, 128, stride=3), :] = turned

    for k in range(n):
        fetch(k).wait()

        def widen(i, carry):
            start = pl.multiple_of(i * 128, 128)
            table_ref[pl.ds(pl.multiple_of(start + (k * chunk + PAD), 8), 128), :] = buf_ref[
                k, pl.ds(start, 128), :
            ].astype(F32)
            return carry

        lax.fori_loop(0, chunk // 128, widen, 0)
    sub = lax.broadcasted_iota(jnp.int32, (8, 128), 0)
    buckets = exc // STEPS
    ids = exc * rows
    at = ids + rows

    front = sub < 3
    back = jnp.logical_and(sub >= 3, sub < 6)

    def make(depth):
        def group(g, carry):
            first = pl.multiple_of(g * WIDE, WIDE)
            near = tgt_ref.at[pl.ds(first, ids + WIDE)]
            w6 = [wt_ref[pl.ds(first * 3 + 6 * q, 8), :] for q in range(WIDE // 2)]
            acc = [jnp.zeros((8, 128), F32)] * (WIDE // 2)
            for e in range(depth):
                for q in range(WIDE // 2):
                    low = table_ref[pl.ds(near[e * rows + 2 * q] + PAD, 8), :]
                    high = table_ref[pl.ds(near[e * rows + 2 * q + 1] + (PAD - 3), 8), :]
                    w = jnp.broadcast_to(w6[q][:, e : e + 1], (8, 128))
                    acc[q] = acc[q] + jnp.where(front, low, high) * w
            for q in range(WIDE // 2):
                low = near[ids + 2 * q] + PAD
                high = near[ids + 2 * q + 1] + (PAD - 3)
                pltpu.store(acc_ref.at[pl.ds(low, 8), :], acc[q], mask=front)
                pltpu.store(acc_ref.at[pl.ds(high, 8), :], acc[q], mask=back)
            return carry

        return group

    for k in reversed(range(buckets)):
        begin = tgt_ref[at + k + 1] if k + 1 < buckets else 0
        lax.fori_loop(begin, tgt_ref[at + k], make((k + 1) * STEPS), 0)

    own = own_ref[0]

    def finish(i, carry):
        for u in range(4):
            place = pl.multiple_of(i * 32 + u * 8, 8)
            for ct in range(3):
                spot = place * 3 + (ct + PAD)
                out_ref[pl.ds(place * 3 + ct, 8, stride=3), :] = (
                    acc_ref[pl.ds(spot, 8, stride=3), :]
                    + diag_ref[pl.ds(place, 8), ct * 128 : (ct + 1) * 128]
                    * table_ref[pl.ds(own * 3 + spot, 8, stride=3), :]
                )
        return carry

    lax.fori_loop(0, rows // 32, finish, 0)


def alpha_term(own, table, numbers, weights, diag, order):
    rows = diag.shape[0]
    total = table.shape[0]
    chunk = total // 8
    return pl.pallas_call(
        alpha_kernel,
        out_shape=jax.ShapeDtypeStruct((rows * 3, 128), F32),
        in_specs=[
            pl.BlockSpec(memory_space=pltpu.SMEM),
            pl.BlockSpec(memory_space=pl.ANY),
            pl.BlockSpec(memory_space=pltpu.SMEM),
            pl.BlockSpec(memory_space=pltpu.VMEM),
            pl.BlockSpec(memory_space=pltpu.VMEM),
            pl.BlockSpec(memory_space=pl.ANY),
        ],
        out_specs=pl.BlockSpec(memory_space=pltpu.VMEM),
        scratch_shapes=[
            pltpu.VMEM((total + 4 * PAD, 128), F32),
            pltpu.VMEM((rows * 3 + PAD, 128), F32),
            pltpu.VMEM((rows * 3 + 4 * PAD, 128), F32),
            pltpu.VMEM((8, chunk, 128), BF16),
            pltpu.SemaphoreType.DMA((8,)),
        ],
        compiler_params=pltpu.CompilerParams(vmem_limit_bytes=VMEM_LIMIT),
        cost_estimate=pl.CostEstimate(
            flops=10**10, bytes_accessed=16 * 2**20, transcendentals=0
        ),
        name="alpha_term",
    )(own, table, numbers, weights, diag, order)


def merge_kernel(nalpha, alpha_ref, beta_ref, out_ref):
    nbeta = beta_ref.shape[0]
    pieces = out_ref.shape[1]

    def senders(beta_s, carry):
        for alpha_s in range(nalpha):
            p = alpha_s * nbeta + beta_s
            one = alpha_ref[pl.ds(p * pieces, pieces), :]
            other = beta_ref[beta_s, alpha_s * pieces : (alpha_s + 1) * pieces, :]
            out_ref[p] = (one + other).astype(BF16)
        return carry

    lax.fori_loop(0, nbeta, senders, 0)


def merge(alpha, beta, nalpha, pieces):
    devices = nalpha * beta.shape[0]
    return pl.pallas_call(
        functools.partial(merge_kernel, nalpha),
        out_shape=jax.ShapeDtypeStruct((devices, pieces, 128), BF16),
        in_specs=[pl.BlockSpec(memory_space=pltpu.VMEM)] * 2,
        out_specs=pl.BlockSpec(memory_space=pltpu.VMEM),
        compiler_params=pltpu.CompilerParams(vmem_limit_bytes=VMEM_LIMIT),
        name="merge",
    )(alpha, beta)


def finish_kernel(entries, parts_ref, sigma_ref, coef_ref, out_ref, rms_ref):
    parts = parts_ref[:, 0, :]
    square = parts[:, 0:1]
    total = jnp.sum(parts, axis=0, keepdims=True)
    rayleigh = total[:, 1:2] / total[:, 0:1]
    shift = rayleigh - parts[:, 3:4]
    rest = jnp.sum(parts[:, 2:3] + shift * shift * square, axis=0, keepdims=True)
    out_ref[...] = sigma_ref[...] - rayleigh * coef_ref[...]
    rms_ref[...] = jnp.sqrt(rest / entries)


def finish(parts, sigma, coef, entries):
    return pl.pallas_call(
        functools.partial(finish_kernel, float(entries)),
        out_shape=(
            jax.ShapeDtypeStruct(sigma.shape, F32),
            jax.ShapeDtypeStruct((1, 1), F32),
        ),
        name="finish",
    )(parts, sigma, coef)


def unpack_kernel(
    r_ref, key_ref, label_ref, coef_ref, tr_ref, sigma_ref, part_ref, stage_ref, half_ref
):
    devices, pieces, _ = r_ref.shape
    rows = devices * pieces // 2
    confs = key_ref.shape[1]
    width = coef_ref.shape[0]
    ncls = tr_ref.shape[0]
    tall = width + -width % 8

    def spread(p, carry):
        stage_ref[pl.ds(p * pieces, pieces), :] = r_ref[p].astype(F32)
        return carry

    lax.fori_loop(0, devices, spread, 0)
    for h in range(2):
        half_ref[:, h * 128 : (h + 1) * 128] = stage_ref[pl.ds(h, rows, stride=2), :].astype(BF16)
    key = key_ref[...]
    block = 256
    dets = jnp.zeros((256, confs), F32)
    for b in range(rows // block):
        onehot = (
            (lax.broadcasted_iota(jnp.int32, (block, confs), 0) + b * block == key)
            .astype(F32)
            .astype(BF16)
        )
        dets = dets + lax.dot_general(
            half_ref[pl.ds(b * block, block), :],
            onehot,
            (((0,), (0,)), ((), ())),
            preferred_element_type=F32,
        )
    trans = jnp.concatenate([padded(tr_ref, c) for c in range(ncls)], axis=0)
    products = jnp.dot(trans, dets, precision=HIGH, preferred_element_type=F32)
    sigma = jnp.zeros((width, confs), F32)
    for c in range(ncls):
        part = products[c * tall : c * tall + width]
        sigma = sigma + jnp.where(label_ref[0:1, :] == c, part, 0.0)
    coef = coef_ref[...]
    sigma_ref[...] = sigma
    square = jnp.sum(jnp.sum(coef * coef, axis=1, keepdims=True), axis=0, keepdims=True)
    cross = jnp.sum(jnp.sum(coef * sigma, axis=1, keepdims=True), axis=0, keepdims=True)
    ratio = jnp.where(square > 0.0, cross / jnp.where(square > 0.0, square, 1.0), 0.0)
    rest = sigma - ratio * coef
    rho = jnp.sum(jnp.sum(rest * rest, axis=1, keepdims=True), axis=0, keepdims=True)
    lane = lax.broadcasted_iota(jnp.int32, (1, 128), 1)
    part = jnp.where(
        lane == 0,
        square,
        jnp.where(lane == 1, cross, jnp.where(lane == 2, rho, jnp.where(lane == 3, ratio, 0.0))),
    )
    part_ref[...] = jnp.broadcast_to(part[None], part_ref.shape)


def unpack(returned, key, labels, coef, transforms):
    return pl.pallas_call(
        unpack_kernel,
        out_shape=(
            jax.ShapeDtypeStruct(coef.shape, F32),
            jax.ShapeDtypeStruct((returned.shape[0], 1, 128), F32),
        ),
        scratch_shapes=[
            pltpu.VMEM((returned.shape[0] * returned.shape[1], 128), F32),
            pltpu.VMEM((returned.shape[0] * returned.shape[1] // 2, 256), BF16),
        ],
        compiler_params=pltpu.CompilerParams(vmem_limit_bytes=VMEM_LIMIT),
        name="unpack",
    )(returned, key, labels, coef, transforms)


def exchange(x, axes):
    return lax.all_to_all(x, axes, split_axis=0, concat_axis=0, tiled=True)


def body(
    csf_coef,
    conf_class,
    conf_tile,
    transforms,
    alpha_targets,
    alpha_values,
    alpha_counts,
    beta_targets,
    beta_values,
    beta_counts,
    det_diag,
):
    nalpha = lax.axis_size("alpha")
    nbeta = lax.axis_size("beta")
    devices = nalpha * nbeta
    ncsf, confs = csf_coef.shape
    capacity = 3 * confs // devices
    rows_alpha = det_diag.shape[0]
    width = transforms.shape[2]
    exc = alpha_targets.shape[0]
    pieces = capacity * width // 128
    labels = jnp.stack([conf_class, conf_tile[:, 0]])
    lists = plan(beta_targets, beta_values, beta_counts, STEPS, FEW, True)
    aplan = plan(alpha_targets, alpha_values, alpha_counts, STEPS, WIDE, False)
    anumbers = jnp.concatenate(
        [
            aplan[:exc] * 384.0 + aplan[exc : 2 * exc] * 3.0,
            aplan[3 * exc : 3 * exc + 1] * 384.0 + aplan[3 * exc + 1 : 3 * exc + 2] * 3.0,
            aplan[3 * exc + 2 : 3 * exc + 3],
        ],
        axis=0,
    )
    anumbers = anumbers.astype(jnp.int32).reshape(-1)
    aweights = aplan[2 * exc : 3 * exc]

    body_rows = nalpha * pieces
    heard = lax.all_gather(lists, "beta", axis=0, tiled=False)
    outgoing, key = pack(csf_coef, labels, transforms, capacity)
    slab = exchange(outgoing.reshape(nalpha, nbeta * pieces, 128), "alpha")
    slab, anumbers, aweights = lax.optimization_barrier((slab, anumbers, aweights))
    x2 = (
        slab.reshape(nalpha, nbeta, pieces, 128)
        .transpose(1, 0, 2, 3)
        .reshape(nbeta, body_rows, 128)
    )
    half = nbeta // 2
    side = lax.axis_index("alpha") % 2
    swap = [(i, i ^ 1) for i in range(nalpha)]
    y2 = lax.ppermute(x2, "alpha", swap)
    btable = slab_table(x2, y2)
    mine = lax.dynamic_slice_in_dim(heard, side * half, half, axis=0)
    bnumbers = mine[:, :64].astype(jnp.int32) * 256 + mine[:, 64:128].astype(jnp.int32) * 2
    sides = side.astype(jnp.int32)[None]

    got = exchange(x2, "beta")
    early = beta_term(sides, btable, bnumbers, heard, body_rows, 0, FIRST, ())
    got, bnumbers, early = lax.optimization_barrier((got, bnumbers, early))
    flat = (
        got.reshape(nbeta, nalpha, pieces, 128).transpose(1, 0, 2, 3).reshape(-1, 128)
    )
    table = lax.all_gather(flat, "alpha", axis=0, tiled=True)
    near, far = beta_term(
        sides, btable, bnumbers, heard, body_rows, FIRST, half - FIRST, tuple(early)
    )
    back = lax.ppermute(far, "alpha", swap)
    beta_slab = lax.dynamic_update_slice(near, back, ((1 - side) * half, 0, 0))
    beta_tile = exchange(beta_slab, "beta")
    own = (lax.axis_index("alpha") * rows_alpha).astype(jnp.int32)[None]
    partial = alpha_term(own, table, anumbers, aweights, det_diag, beta_slab)
    sigma_tile = merge(partial, beta_tile, nalpha, pieces)
    returned = exchange(sigma_tile, BOTH)
    sigma, part = unpack(returned, key, labels, csf_coef, transforms)
    parts = exchange(part, BOTH)
    residual, rms = finish(parts, sigma, csf_coef, ncsf * confs * devices)
    return (residual, rms[0, 0])


def solution(mesh):
    placed = (
        P(None, BOTH),
        P(BOTH),
        P(BOTH, None),
        P(),
        P(None, "alpha"),
        P(None, "alpha"),
        P("alpha"),
        P(None, "beta"),
        P(None, "beta"),
        P("beta"),
        P("alpha", "beta"),
    )
    return jax.shard_map(
        body,
        mesh=mesh,
        in_specs=placed,
        out_specs=(P(None, BOTH), P()),
        check_vma=False,
    )
```

```python
import functools

import jax
import jax.numpy as jnp
from jax import lax
from jax.experimental import pallas as pl
from jax.experimental.pallas import tpu as pltpu
from jax.sharding import PartitionSpec as P


F32 = jnp.float32
BF16 = jnp.bfloat16
HIGH = lax.Precision.HIGHEST
BOTH = ("alpha", "beta")
PAD = 8
FIRST = 1
STEPS = 2
WIDE = 32
FEW = 16
VMEM_LIMIT = 60 * 1024 * 1024


def stacked(coef, classes, classes_n):
    parts = []
    for c in range(classes_n):
        parts.append(jnp.where(classes == c, coef, jnp.zeros_like(coef)))
    return jnp.concatenate(parts, axis=0)


def padded(ref, index=None):
    value = ref[...] if index is None else ref[index]
    fill = -value.shape[0] % 8
    return jnp.concatenate([value, jnp.zeros((fill, value.shape[1]), F32)], axis=0)


def pack_kernel(capacity, coef_ref, class_ref, tile_ref, tr_ref, out_ref, key_ref, inter_ref):
    confs = coef_ref.shape[1]
    ncls = tr_ref.shape[0]
    devices = confs * 3 // capacity
    masked = stacked(padded(coef_ref), class_ref[...], ncls)
    trans = jnp.concatenate([padded(tr_ref, c) for c in range(ncls)], axis=0)
    dets = lax.dot_general(
        masked, trans, (((0,), (0,)), ((), ())), precision=HIGH, preferred_element_type=F32
    ).astype(BF16)
    tile = tile_ref[...]
    hit = lax.broadcasted_iota(jnp.int32, (devices, confs), 0) == tile
    before = lax.broadcasted_iota(jnp.int32, (confs, confs), 0) < lax.broadcasted_iota(
        jnp.int32, (confs, confs), 1
    )
    counts = jnp.dot(
        hit.astype(F32).astype(BF16), before.astype(F32).astype(BF16), preferred_element_type=F32
    )
    slot = jnp.sum(jnp.where(hit, counts, 0.0), axis=0, keepdims=True).astype(jnp.int32)
    key = tile * capacity + slot
    key_ref[...] = key
    rows = devices * capacity
    block = 256
    for b in range(rows // block):
        onehot = (
            (lax.broadcasted_iota(jnp.int32, (block, confs), 0) + b * block == key)
            .astype(F32)
            .astype(BF16)
        )
        picked = jnp.dot(onehot, dets, preferred_element_type=F32)
        for h in range(2):
            inter_ref[pl.ds(h, block, stride=2), :] = picked[:, h * 128 : (h + 1) * 128]
        out_ref[pl.ds(b * 2 * block, 2 * block), :] = inter_ref[...].astype(BF16)


def pack(coef, classes, tiles, transforms, capacity):
    confs = coef.shape[1]
    rows = 2 * 3 * confs
    return pl.pallas_call(
        functools.partial(pack_kernel, capacity),
        out_shape=(
            jax.ShapeDtypeStruct((rows, 128), BF16),
            jax.ShapeDtypeStruct((1, confs), jnp.int32),
        ),
        scratch_shapes=[pltpu.VMEM((512, 128), F32)],
        compiler_params=pltpu.CompilerParams(vmem_limit_bytes=VMEM_LIMIT),
        name="pack",
    )(coef, classes, tiles, transforms)


def build_table(slab_refs, table_ref, stage_ref):
    blocks, rows, _ = slab_refs[0].shape
    lanes = rows // 3

    def build(j, carry):
        for h, slab_ref in enumerate(slab_refs):
            stage_ref[...] = slab_ref[j].astype(F32)
            for ct in range(3):
                piece = stage_ref[pl.ds(ct, lanes, stride=3), :]
                piece = jnp.concatenate([piece, jnp.zeros((128 - lanes, 128), F32)], axis=0)
                start = (j * 3 + ct) * 256 + (PAD + h)
                table_ref[pl.ds(start, 128, stride=2), :] = piece.T
        return carry

    lax.fori_loop(0, blocks, build, 0)


def plan_kernel(steps, width, tgt_ref, val_ref, cnt_ref, out_ref, *row_refs):
    exc, length = tgt_ref.shape
    counts = cnt_ref[...]
    place = lax.broadcasted_iota(jnp.int32, (1, length), 1)
    key = counts * 4096 + (4095 - place)
    key8 = jnp.broadcast_to(key, (8, length)).astype(F32)
    slots = lax.broadcasted_iota(jnp.int32, (exc, length), 0)
    live = jnp.where(slots < counts, val_ref[...].astype(F32), 0.0)
    tgt = tgt_ref[...]
    high = tgt >> 7
    rows = lax.broadcasted_iota(jnp.int32, (8, length), 0)
    extra = jnp.where(rows == 0, place >> 7, jnp.where(rows == 1, place & 127, 0))
    lists = jnp.concatenate(
        [high.astype(F32), (tgt & 127).astype(F32), live, extra.astype(F32)], axis=0
    ).astype(BF16)
    total = jnp.zeros((lists.shape[0], length), F32)
    for k in range(length // 128):
        mine = key8[:, k * 128 : (k + 1) * 128]
        column = jnp.concatenate([mine] * 16, axis=0).T[:, 0:1]
        ahead = jnp.where(key8[0:1, :] > column, 1.0, 0.0)
        rank = jnp.sum(ahead, axis=1, keepdims=True).astype(jnp.int32)
        moved = (
            (lax.broadcasted_iota(jnp.int32, (128, length), 1) == rank).astype(F32).astype(BF16)
        )
        total = total + jnp.dot(
            lists[:, k * 128 : (k + 1) * 128], moved, preferred_element_type=F32
        )
    lane = lax.broadcasted_iota(jnp.int32, (8, length), 1)
    bounds = jnp.zeros((8, length), F32)
    for k in range(exc // steps):
        over = jnp.sum(jnp.where(counts > k * steps, 1.0, 0.0), axis=1, keepdims=True)
        groups = ((over.astype(jnp.int32) + (width - 1)) // width).astype(F32)
        bounds = jnp.where(jnp.logical_and(lane == k, rows == 2), groups, bounds)
    tail = jnp.where(rows == 2, bounds, total[3 * exc :])
    if not row_refs:
        out_ref[0 : 3 * exc, :] = total[: 3 * exc]
        out_ref[3 * exc :, :] = tail
        return
    (row_ref,) = row_refs
    row_ref[...] = jnp.zeros_like(row_ref)
    parts = length // 128
    for ct in range(parts):
        lanes = slice(ct * 128, (ct + 1) * 128)
        for k in range(3):
            row_ref[pl.ds(k * 64 + ct, exc, stride=parts), :] = total[
                k * exc : (k + 1) * exc, lanes
            ]
        high_row = exc * parts + ct
        row_ref[high_row : high_row + 1, :] = tail[0:1, lanes]
        row_ref[64 + high_row : 65 + high_row, :] = tail[1:2, lanes]
        bound_row = 64 + (exc + 1) * parts + ct
        row_ref[bound_row : bound_row + 1, :] = tail[2:3, lanes]
    out_ref[...] = row_ref[...].astype(BF16)


def plan(targets, values, counts, steps, width, packed):
    exc, length = targets.shape
    wanted = jax.ShapeDtypeStruct((3 * exc + 8, length), F32)
    return pl.pallas_call(
        functools.partial(plan_kernel, steps, width),
        out_shape=jax.ShapeDtypeStruct((256, 128), BF16) if packed else wanted,
        scratch_shapes=[pltpu.VMEM((256, 128), F32)] if packed else [],
        compiler_params=pltpu.CompilerParams(vmem_limit_bytes=VMEM_LIMIT),
        name="plan",
    )(targets, values, counts[None, :])


def beta_block(table_ref, tgt_ref, row_ref, w_ref, out_refs, wt_ref, acc_ref, wide_ref):
    lanes = out_refs[0].shape[1] // 3
    exc = 16
    cols = 384
    slot = lax.broadcasted_iota(jnp.int32, (8, 128), 0) >> 1
    wide_ref[...] = w_ref[0].astype(F32)
    for ct in range(3):
        turned = jnp.concatenate(
            [wide_ref[pl.ds(ct, exc, stride=3), :], jnp.zeros((128 - exc, 128), F32)], axis=0
        ).T
        for h in range(2):
            wt_ref[pl.ds(ct * 256 + h, 128, stride=2), :] = turned
    buckets = exc // STEPS
    at = (exc + 1) * cols

    def make(depth):
        def group(g, carry):
            near = tgt_ref.at[pl.ds(g * FEW, exc * cols)]
            for v in range(FEW // 4):
                first = pl.multiple_of(g * (2 * FEW) + v * 8, 8)
                w8 = wt_ref[pl.ds(first, 8), :]
                acc = jnp.zeros((8, 128), F32)
                for e in range(depth):
                    got = None
                    for s in range(4):
                        t = near[e * cols + 4 * v + s]
                        win = table_ref[pl.ds(t + (PAD - 2 * s), 8), :]
                        got = win if s == 0 else jnp.where(slot == s, win, got)
                    acc = acc + got * w8[:, e : e + 1]
                acc_ref[pl.ds(first, 8), :] = acc
            return carry

        return group

    for k in reversed(range(buckets)):
        begin = tgt_ref[at + k + 1] >> 1 if k + 1 < buckets else 0
        lax.fori_loop(begin, tgt_ref[at + k] >> 1, make((k + 1) * STEPS), 0)
    ids = jnp.concatenate([row_ref[0, exc * 3 + ct : exc * 3 + ct + 1, :] for ct in range(3)], axis=1)
    back = (
        (lax.broadcasted_iota(jnp.int32, (cols, cols), 0) * 2 == ids).astype(F32).astype(BF16)
    )
    for h, out_ref in enumerate(out_refs):
        left = acc_ref[pl.ds(h, cols, stride=2), :].T
        done = jnp.zeros((128, cols), F32)
        for _ in range(3):
            piece = left.astype(BF16)
            done = done + lax.dot_general(
                piece, back, (((1,), (1,)), ((), ())), preferred_element_type=F32
            )
            left = left - piece.astype(F32)
        for ct in range(3):
            out_ref[0, pl.ds(ct, lanes, stride=3), :] = done[:lanes, ct * 128 : (ct + 1) * 128]


def table_kernel(x_ref, y_ref, table_ref, stage_ref):
    build_table((x_ref, y_ref), table_ref, stage_ref)


def slab_table(x2, y2):
    nbeta, rows, _ = x2.shape
    return pl.pallas_call(
        table_kernel,
        out_shape=jax.ShapeDtypeStruct((2 * nbeta * 384 + 2 * PAD, 128), F32),
        in_specs=[pl.BlockSpec(memory_space=pltpu.VMEM)] * 2,
        out_specs=pl.BlockSpec(memory_space=pltpu.VMEM),
        scratch_shapes=[pltpu.VMEM((rows, 128), F32)],
        compiler_params=pltpu.CompilerParams(vmem_limit_bytes=VMEM_LIMIT),
        cost_estimate=pl.CostEstimate(flops=10**9, bytes_accessed=2**23, transcendentals=0),
        name="slab_table",
    )(x2, y2)


def beta_kernel(side_ref, table_ref, tgt_ref, row_ref, w_ref, *refs):
    own_ref, far_ref, wt_ref, acc_ref, wide_ref = refs[-5:]
    beta_block(
        table_ref, tgt_ref, row_ref, w_ref, (own_ref, far_ref), wt_ref, acc_ref, wide_ref
    )


def beta_term(side, table, numbers, heard, rows, skip, blocks, old):
    half = numbers.shape[0]
    nbeta = heard.shape[0]
    near = pl.BlockSpec((1, rows, 128), lambda j, side: (side[0] * half + j + skip, 0, 0))
    far = pl.BlockSpec((1, rows, 128), lambda j, side: (j + skip, 0, 0))
    return pl.pallas_call(
        beta_kernel,
        out_shape=(
            jax.ShapeDtypeStruct((nbeta, rows, 128), F32),
            jax.ShapeDtypeStruct((half, rows, 128), F32),
        ),
        grid_spec=pltpu.PrefetchScalarGridSpec(
            num_scalar_prefetch=1,
            grid=(blocks,),
            in_specs=[
                pl.BlockSpec(table.shape, lambda j, side: (0, 0)),
                pl.BlockSpec((8192,), lambda j, side: (j + skip,), memory_space=pltpu.SMEM),
                pl.BlockSpec((1, 64, 128), lambda j, side: (j + skip, 0, 0)),
                pl.BlockSpec((1, 64, 128), lambda j, side: (side[0] * half + j + skip, 2, 0)),
            ]
            + [pl.BlockSpec(memory_space=pl.ANY)] * len(old),
            out_specs=(near, far),
            scratch_shapes=[
                pltpu.VMEM((768, 128), F32),
                pltpu.VMEM((768, 128), F32),
                pltpu.VMEM((64, 128), F32),
            ],
        ),
        input_output_aliases={5: 0, 6: 1} if old else {},
        compiler_params=pltpu.CompilerParams(vmem_limit_bytes=VMEM_LIMIT),
        cost_estimate=pl.CostEstimate(
            flops=blocks * 8 * 10**8, bytes_accessed=blocks * 2**20, transcendentals=0
        ),
        name="beta_rest" if old else "beta_first",
    )(side, table, numbers.reshape(-1), numbers, heard, *old)


def alpha_kernel(
    own_ref,
    tbl_hbm,
    tgt_ref,
    w_ref,
    diag_ref,
    order_ref,
    out_ref,
    table_ref,
    wt_ref,
    acc_ref,
    buf_ref,
    sem,
):
    chunk = buf_ref.shape[1]
    total = tbl_hbm.shape[0]
    n = total // chunk
    exc = w_ref.shape[0]
    rows = diag_ref.shape[0]

    def fetch(k):
        return pltpu.make_async_copy(
            tbl_hbm.at[pl.ds(k * chunk, chunk), :], buf_ref.at[k], sem.at[k]
        )

    for k in range(n):
        fetch(k).start()
    for k in range(rows // 128):
        turned = jnp.concatenate(
            [w_ref[:, k * 128 : (k + 1) * 128], jnp.zeros((128 - exc, 128), F32)], axis=0
        ).T
        for ct in range(3):
            wt_ref[pl.ds(k * 384 + ct, 128, stride=3), :] = turned

    for k in range(n):
        fetch(k).wait()

        def widen(i, carry):
            start = pl.multiple_of(i * 128, 128)
            table_ref[pl.ds(pl.multiple_of(start + (k * chunk + PAD), 8), 128), :] = buf_ref[
                k, pl.ds(start, 128), :
            ].astype(F32)
            return carry

        lax.fori_loop(0, chunk // 128, widen, 0)
    sub = lax.broadcasted_iota(jnp.int32, (8, 128), 0)
    buckets = exc // STEPS
    ids = exc * rows
    at = ids + rows

    front = sub < 3
    back = jnp.logical_and(sub >= 3, sub < 6)

    def make(depth):
        def group(g, carry):
            first = pl.multiple_of(g * WIDE, WIDE)
            near = tgt_ref.at[pl.ds(first, ids + WIDE)]
            w6 = [wt_ref[pl.ds(first * 3 + 6 * q, 8), :] for q in range(WIDE // 2)]
            acc = [jnp.zeros((8, 128), F32)] * (WIDE // 2)
            for e in range(depth):
                for q in range(WIDE // 2):
                    low = table_ref[pl.ds(near[e * rows + 2 * q] + PAD, 8), :]
                    high = table_ref[pl.ds(near[e * rows + 2 * q + 1] + (PAD - 3), 8), :]
                    w = jnp.broadcast_to(w6[q][:, e : e + 1], (8, 128))
                    acc[q] = acc[q] + jnp.where(front, low, high) * w
            for q in range(WIDE // 2):
                low = near[ids + 2 * q] + PAD
                high = near[ids + 2 * q + 1] + (PAD - 3)
                pltpu.store(acc_ref.at[pl.ds(low, 8), :], acc[q], mask=front)
                pltpu.store(acc_ref.at[pl.ds(high, 8), :], acc[q], mask=back)
            return carry

        return group

    for k in reversed(range(buckets)):
        begin = tgt_ref[at + k + 1] if k + 1 < buckets else 0
        lax.fori_loop(begin, tgt_ref[at + k], make((k + 1) * STEPS), 0)

    own = own_ref[0]

    def finish(i, carry):
        for u in range(4):
            place = pl.multiple_of(i * 32 + u * 8, 8)
            for ct in range(3):
                spot = place * 3 + (ct + PAD)
                out_ref[pl.ds(place * 3 + ct, 8, stride=3), :] = (
                    acc_ref[pl.ds(spot, 8, stride=3), :]
                    + diag_ref[pl.ds(place, 8), ct * 128 : (ct + 1) * 128]
                    * table_ref[pl.ds(own * 3 + spot, 8, stride=3), :]
                )
        return carry

    lax.fori_loop(0, rows // 32, finish, 0)


def alpha_term(own, table, numbers, weights, diag, order):
    rows = diag.shape[0]
    total = table.shape[0]
    chunk = total // 8
    return pl.pallas_call(
        alpha_kernel,
        out_shape=jax.ShapeDtypeStruct((rows * 3, 128), F32),
        in_specs=[
            pl.BlockSpec(memory_space=pltpu.SMEM),
            pl.BlockSpec(memory_space=pl.ANY),
            pl.BlockSpec(memory_space=pltpu.SMEM),
            pl.BlockSpec(memory_space=pltpu.VMEM),
            pl.BlockSpec(memory_space=pltpu.VMEM),
            pl.BlockSpec(memory_space=pl.ANY),
        ],
        out_specs=pl.BlockSpec(memory_space=pltpu.VMEM),
        scratch_shapes=[
            pltpu.VMEM((total + 4 * PAD, 128), F32),
            pltpu.VMEM((rows * 3 + PAD, 128), F32),
            pltpu.VMEM((rows * 3 + 4 * PAD, 128), F32),
            pltpu.VMEM((8, chunk, 128), BF16),
            pltpu.SemaphoreType.DMA((8,)),
        ],
        compiler_params=pltpu.CompilerParams(vmem_limit_bytes=VMEM_LIMIT),
        cost_estimate=pl.CostEstimate(
            flops=10**10, bytes_accessed=16 * 2**20, transcendentals=0
        ),
        name="alpha_term",
    )(own, table, numbers, weights, diag, order)


def merge_kernel(nalpha, alpha_ref, beta_ref, out_ref):
    devices, pieces, _ = out_ref.shape
    nbeta = devices // nalpha

    def senders(beta_s, carry):
        for alpha_s in range(nalpha):
            p = alpha_s * nbeta + beta_s
            q = beta_s * nalpha + alpha_s
            one = alpha_ref[pl.ds(p * pieces, pieces), :]
            other = beta_ref[pl.ds(q * pieces, pieces), :]
            out_ref[p] = (one + other).astype(BF16)
        return carry

    lax.fori_loop(0, nbeta, senders, 0)


def merge(alpha, beta, nalpha, devices):
    return pl.pallas_call(
        functools.partial(merge_kernel, nalpha),
        out_shape=jax.ShapeDtypeStruct((devices, alpha.shape[0] // devices, 128), BF16),
        in_specs=[pl.BlockSpec(memory_space=pltpu.VMEM)] * 2,
        out_specs=pl.BlockSpec(memory_space=pltpu.VMEM),
        compiler_params=pltpu.CompilerParams(vmem_limit_bytes=16 * 2**20),
        name="merge",
    )(alpha, beta)


def finish_kernel(entries, parts_ref, sigma_ref, coef_ref, out_ref, rms_ref):
    parts = parts_ref[:, 0, :]
    square = parts[:, 0:1]
    total = jnp.sum(parts, axis=0, keepdims=True)
    rayleigh = total[:, 1:2] / total[:, 0:1]
    shift = rayleigh - parts[:, 3:4]
    rest = jnp.sum(parts[:, 2:3] + shift * shift * square, axis=0, keepdims=True)
    out_ref[...] = sigma_ref[...] - rayleigh * coef_ref[...]
    rms_ref[...] = jnp.sqrt(rest / entries)


def finish(parts, sigma, coef, entries):
    return pl.pallas_call(
        functools.partial(finish_kernel, float(entries)),
        out_shape=(
            jax.ShapeDtypeStruct(sigma.shape, F32),
            jax.ShapeDtypeStruct((1, 1), F32),
        ),
        name="finish",
    )(parts, sigma, coef)


def unpack_kernel(
    r_ref, key_ref, class_ref, coef_ref, tr_ref, sigma_ref, part_ref, stage_ref, half_ref
):
    devices, pieces, _ = r_ref.shape
    rows = devices * pieces // 2
    confs = key_ref.shape[1]
    width = coef_ref.shape[0]
    ncls = tr_ref.shape[0]
    tall = width + -width % 8

    def spread(i, carry):
        for u in range(8):
            p = i * 8 + u
            stage_ref[pl.ds(p * pieces, pieces), :] = r_ref[p].astype(F32)
        return carry

    lax.fori_loop(0, devices // 8, spread, 0)
    for h in range(2):
        half_ref[:, h * 128 : (h + 1) * 128] = stage_ref[pl.ds(h, rows, stride=2), :].astype(BF16)
    key = key_ref[...]
    block = 256
    dets = jnp.zeros((256, confs), F32)
    for b in range(rows // block):
        onehot = (
            (lax.broadcasted_iota(jnp.int32, (block, confs), 0) + b * block == key)
            .astype(F32)
            .astype(BF16)
        )
        dets = dets + lax.dot_general(
            half_ref[pl.ds(b * block, block), :],
            onehot,
            (((0,), (0,)), ((), ())),
            preferred_element_type=F32,
        )
    trans = jnp.concatenate([padded(tr_ref, c) for c in range(ncls)], axis=0)
    products = jnp.dot(trans, dets, precision=HIGH, preferred_element_type=F32)
    sigma = jnp.zeros((width, confs), F32)
    for c in range(ncls):
        part = products[c * tall : c * tall + width]
        sigma = sigma + jnp.where(class_ref[...] == c, part, 0.0)
    coef = coef_ref[...]
    sigma_ref[...] = sigma
    square = jnp.sum(jnp.sum(coef * coef, axis=1, keepdims=True), axis=0, keepdims=True)
    cross = jnp.sum(jnp.sum(coef * sigma, axis=1, keepdims=True), axis=0, keepdims=True)
    ratio = jnp.where(square > 0.0, cross / jnp.where(square > 0.0, square, 1.0), 0.0)
    rest = sigma - ratio * coef
    rho = jnp.sum(jnp.sum(rest * rest, axis=1, keepdims=True), axis=0, keepdims=True)
    lane = lax.broadcasted_iota(jnp.int32, (1, 128), 1)
    part = jnp.where(
        lane == 0,
        square,
        jnp.where(lane == 1, cross, jnp.where(lane == 2, rho, jnp.where(lane == 3, ratio, 0.0))),
    )
    part_ref[...] = jnp.broadcast_to(part[None], part_ref.shape)


def unpack(returned, key, classes, coef, transforms):
    return pl.pallas_call(
        unpack_kernel,
        out_shape=(
            jax.ShapeDtypeStruct(coef.shape, F32),
            jax.ShapeDtypeStruct((returned.shape[0], 1, 128), F32),
        ),
        scratch_shapes=[
            pltpu.VMEM((returned.shape[0] * returned.shape[1], 128), F32),
            pltpu.VMEM((returned.shape[0] * returned.shape[1] // 2, 256), BF16),
        ],
        compiler_params=pltpu.CompilerParams(vmem_limit_bytes=VMEM_LIMIT),
        name="unpack",
    )(returned, key, classes, coef, transforms)


def exchange(x, axes):
    return lax.all_to_all(x, axes, split_axis=0, concat_axis=0, tiled=True)


def body(
    csf_coef,
    conf_class,
    conf_tile,
    transforms,
    alpha_targets,
    alpha_values,
    alpha_counts,
    beta_targets,
    beta_values,
    beta_counts,
    det_diag,
):
    nalpha = lax.axis_size("alpha")
    nbeta = lax.axis_size("beta")
    devices = nalpha * nbeta
    ncsf, confs = csf_coef.shape
    capacity = 3 * confs // devices
    rows_alpha = det_diag.shape[0]
    width = transforms.shape[2]
    exc = alpha_targets.shape[0]
    pieces = capacity * width // 128
    classes = conf_class[None, :]
    tiles = conf_tile.reshape(1, -1)
    lists = plan(beta_targets, beta_values, beta_counts, STEPS, FEW, True)
    aplan = plan(alpha_targets, alpha_values, alpha_counts, STEPS, WIDE, False)
    anumbers = jnp.concatenate(
        [
            aplan[:exc] * 384.0 + aplan[exc : 2 * exc] * 3.0,
            aplan[3 * exc : 3 * exc + 1] * 384.0 + aplan[3 * exc + 1 : 3 * exc + 2] * 3.0,
            aplan[3 * exc + 2 : 3 * exc + 3],
        ],
        axis=0,
    )
    anumbers = anumbers.astype(jnp.int32).reshape(-1)
    aweights = aplan[2 * exc : 3 * exc]

    body_rows = nalpha * pieces
    heard = lax.all_gather(lists, "beta", axis=0, tiled=False)
    outgoing, key = pack(csf_coef, classes, tiles, transforms, capacity)
    slab = exchange(outgoing.reshape(nalpha, nbeta * pieces, 128), "alpha")
    slab, anumbers, aweights = lax.optimization_barrier((slab, anumbers, aweights))
    x2 = (
        slab.reshape(nalpha, nbeta, pieces, 128)
        .transpose(1, 0, 2, 3)
        .reshape(nbeta, body_rows, 128)
    )
    half = nbeta // 2
    side = lax.axis_index("alpha") % 2
    swap = [(i, i ^ 1) for i in range(nalpha)]
    y2 = lax.ppermute(x2, "alpha", swap)
    btable = slab_table(x2, y2)
    mine = lax.dynamic_slice_in_dim(heard, side * half, half, axis=0)
    bnumbers = mine[:, :64].astype(jnp.int32) * 256 + mine[:, 64:128].astype(jnp.int32) * 2
    sides = side.astype(jnp.int32)[None]

    got = exchange(x2, "beta")
    early = beta_term(sides, btable, bnumbers, heard, body_rows, 0, FIRST, ())
    got, bnumbers, early = lax.optimization_barrier((got, bnumbers, early))
    flat = (
        got.reshape(nbeta, nalpha, pieces, 128).transpose(1, 0, 2, 3).reshape(-1, 128)
    )
    table = lax.all_gather(flat, "alpha", axis=0, tiled=True)
    near, far = beta_term(
        sides, btable, bnumbers, heard, body_rows, FIRST, half - FIRST, tuple(early)
    )
    back = lax.ppermute(far, "alpha", swap)
    beta_slab = lax.dynamic_update_slice(near, back, ((1 - side) * half, 0, 0))
    beta_tile = exchange(beta_slab, "beta")
    own = (lax.axis_index("alpha") * rows_alpha).astype(jnp.int32)[None]
    partial = alpha_term(own, table, anumbers, aweights, det_diag, beta_slab[0, :8])
    sigma_tile = merge(partial, beta_tile.reshape(-1, 128), nalpha, devices)
    returned = exchange(sigma_tile, BOTH)
    sigma, part = unpack(returned, key, classes, csf_coef, transforms)
    parts = exchange(part, BOTH)
    residual, rms = finish(parts, sigma, csf_coef, ncsf * confs * devices)
    return (residual, rms[0, 0])


def solution(mesh):
    placed = (
        P(None, BOTH),
        P(BOTH),
        P(BOTH, None),
        P(),
        P(None, "alpha"),
        P(None, "alpha"),
        P("alpha"),
        P(None, "beta"),
        P(None, "beta"),
        P("beta"),
        P("alpha", "beta"),
    )
    return jax.shard_map(
        body,
        mesh=mesh,
        in_specs=placed,
        out_specs=(P(None, BOTH), P()),
        check_vma=False,
    )
```
